32 devices in a mesh: group: 2 (over x), sec: 16 (over z, y, core).
Axes of the slice: x: 2, y: 2, z: 4, core: 2. Of those that a mesh axis runs over, the one named last changes fastest.
Arguments:
- patches: bfloat16 [32, 128, 128, 128], P(('group', 'sec')), parts along dimension 0, may hold values from -24 to 24
- pair_list: int32 [32, 64], P(('group', 'sec')), parts along dimension 0, may hold values from 0 to 127, as said below
- pair_count: int32 [32], P(('group', 'sec')), parts along dimension 0, may hold values from 0 to 64, as said below
- tissue: int32 [32, 128], P(('group', 'sec')), parts along dimension 0, may hold values 0 or 1
Outputs:
- pair_flow: float32 [32, 2, 64], P(('group', 'sec')), parts along dimension 0
- positions: float32 [32, 2, 128], P(('group', 'sec')), parts along dimension 0
The draws below stay inside these ranges and needn't reach their ends.
There are 2 independent parts, one for each index of `group`. The reference program is written for one: setup_inputs(seed, part) draws one part's arguments, and reference() takes and returns one part's arrays. A program takes and returns all parts, laid end to end along the dimension named above; each array names one. Nothing has to cross between parts.
Inputs may be any that keep to these rules, and one draw needn't show every extreme that they name: `pair_list`: the first pair_count[s] entries of row s are distinct patch indices; the other entries are 0. `pair_count`: some section other than the last has exactly 64 live slots; the last section has 0.
All inputs are finite; a program needn't handle non-finite values. No bound on the sum of `tissue` on one device may be relied on, other than what follows from the above.
Results may differ from the reference program's by a relative error of at most 0.0029.
Values may be sent and summed in bfloat16 or wider, within the bound.
A program may use at most 64 MiB of HBM per device.

```python
import jax
import jax.numpy as jnp
from jax import lax

PS = 128
GR = 8
ITERS = 3
P_SIZE = 128
LIST = 64
SEC = 16


def shift_image(image, down_by, right_by):
    return jnp.roll(jnp.roll(image, down_by, axis=0), right_by, axis=1)


def draw_patches(key, part):
    base_field = jax.random.normal(jax.random.fold_in(key, 1), (P_SIZE, PS, PS), jnp.float32)
    reach = 3 * PS // 8
    offsets = jax.random.randint(jax.random.fold_in(key, 2), (SEC, P_SIZE, 2), -reach, reach + 1)
    toward = jax.random.randint(jax.random.fold_in(key, 3), (SEC, P_SIZE), 0, 2)
    uneven = jax.random.uniform(jax.random.fold_in(key, 4), (SEC, P_SIZE), jnp.float32, 0.015, 0.045)
    noise_keys = jax.random.split(jax.random.fold_in(key, 5), SEC)
    moved_images = jax.vmap(shift_image)

    def advance(earlier, section_inputs):
        offset_pair, side_pick, spread, noise_key = section_inputs
        primary = moved_images(earlier, offset_pair[:, 0], offset_pair[:, 1])
        second = moved_images(earlier, offset_pair[:, 0] + side_pick, offset_pair[:, 1] + 1 - side_pick)
        noise_part = jax.random.normal(noise_key, (P_SIZE, PS, PS), jnp.float32)
        new_field = 0.5 * primary + (0.5 - spread)[:, None, None] * second + 0.7 * noise_part
        return (new_field, new_field)
    final_field, rest_fields = lax.scan(advance, base_field, (offsets[:-1], toward[:-1], uneven[:-1], noise_keys[:-1]))
    stacked = jnp.concatenate([base_field[None], rest_fields], axis=0)
    faint_order = jax.random.permutation(jax.random.fold_in(key, 7), P_SIZE)
    faint_scale = jnp.where(faint_order < P_SIZE // 4, 0.15, 1.0).astype(jnp.float32)
    stacked = stacked * faint_scale[None, :, None, None]
    return jnp.clip(stacked, -24.0, 24.0).astype(jnp.bfloat16)


def permute_one(subkey):
    return jax.random.permutation(subkey, P_SIZE)


def list_helper(key):
    lowest = max(1, LIST // 8)
    highest = min(LIST, max(2, LIST // 2))
    counts = jax.random.randint(jax.random.fold_in(key, 11), (SEC,), lowest, highest + 1)
    busiest = jax.random.randint(jax.random.fold_in(key, 12), (), 0, SEC - 1)
    section_index = jnp.arange(SEC)
    counts = jnp.where(section_index == busiest, LIST, counts)
    counts = jnp.where(section_index == SEC - 1, 0, counts)
    orders = jax.vmap(permute_one)(jax.random.split(jax.random.fold_in(key, 13), SEC))
    slot_index = jnp.arange(LIST)
    listing = jnp.where(slot_index[None, :] < counts[:, None], orders[:, :LIST], 0)
    return (listing.astype(jnp.int32), counts.astype(jnp.int32))


def draw_pair_list(key, part):
    listing, counts = list_helper(key)
    return listing


def draw_pair_count(key, part):
    listing, counts = list_helper(key)
    return counts


def set_ends(drawn, own_key, least, top_value):
    dims = drawn.shape
    index_at = [jax.random.randint(jax.random.fold_in(own_key, axis), (), 0, dims[axis]) for axis in range(len(dims))]
    drawn = drawn.at[tuple(index_at)].set(least)
    longest = dims.index(max(dims))
    index_at[longest] = (index_at[longest] + 1) % dims[longest]
    return drawn.at[tuple(index_at)].set(top_value)


def setup_inputs(seed: int = 0, part: int = 0) -> dict:
    splits = jax.random.split(jax.random.key(seed), 5)
    part_splits = jax.random.split(jax.random.fold_in(splits[4], part), 5)
    return {
        "patches": draw_patches(jax.random.fold_in(jax.random.fold_in(splits[4], part), 71), part),
        "pair_list": draw_pair_list(jax.random.fold_in(jax.random.fold_in(splits[4], part), 71), part),
        "pair_count": draw_pair_count(jax.random.fold_in(jax.random.fold_in(splits[4], part), 71), part),
        "tissue": set_ends((jax.random.randint(part_splits[3], (SEC, P_SIZE), 0, 2) < 1).astype(jnp.int32), jax.random.fold_in(part_splits[3], 1), 0, 1),
    }


spring_rate = 0.25
step_rate = 0.15


def dft_tables(length):
    index = jnp.arange(length, dtype=jnp.int32)
    product = (index[:, None] * index[None, :]) % length
    angle_grid = product.astype(jnp.float32) * (2.0 * jnp.pi / length)
    return jnp.cos(angle_grid).astype(jnp.bfloat16), jnp.sin(angle_grid).astype(jnp.bfloat16)


def right_mul(patch_block, dft_table):
    return jnp.einsum('lxy,yk->lxk', patch_block.astype(jnp.float32), dft_table.astype(jnp.float32), precision=lax.Precision.HIGHEST)


def left_mul(dft_table, patch_block):
    return jnp.einsum('kx,lxy->lky', dft_table.astype(jnp.float32), patch_block.astype(jnp.float32), precision=lax.Precision.HIGHEST)


def spectrum_pair(patch_block, cosine_table, sine_table):
    with_cos = right_mul(patch_block, cosine_table).astype(jnp.bfloat16)
    with_sin = right_mul(patch_block, sine_table).astype(jnp.bfloat16)
    real_part = (left_mul(cosine_table, with_cos) - left_mul(sine_table, with_sin)).astype(jnp.bfloat16)
    imag_part = (-(left_mul(cosine_table, with_sin) + left_mul(sine_table, with_cos))).astype(jnp.bfloat16)
    return real_part.astype(jnp.float32), imag_part.astype(jnp.float32)


def soft_peak(lower_block, upper_block, cosine_table, sine_table):
    lower_real, lower_imag = spectrum_pair(lower_block, cosine_table, sine_table)
    upper_real, upper_imag = spectrum_pair(upper_block, cosine_table, sine_table)
    cross_real = (lower_real * upper_real + lower_imag * upper_imag).astype(jnp.bfloat16)
    cross_imag = (lower_real * upper_imag - lower_imag * upper_real).astype(jnp.bfloat16)
    inner_real = (right_mul(cross_real, cosine_table) - right_mul(cross_imag, sine_table)).astype(jnp.bfloat16)
    inner_imag = (right_mul(cross_real, sine_table) + right_mul(cross_imag, cosine_table)).astype(jnp.bfloat16)
    raw_corr = left_mul(cosine_table, inner_real) - left_mul(sine_table, inner_imag)
    side_length = raw_corr.shape[-1]
    scores = raw_corr * (64.0 / float(side_length * side_length * side_length * side_length))
    weights = jax.nn.softmax(scores.reshape(raw_corr.shape[0], -1), axis=-1).reshape(raw_corr.shape)
    lag_values = ((jnp.arange(side_length) + side_length // 2) % side_length - side_length // 2).astype(jnp.float32)
    shift_rows = jnp.sum(jnp.sum(weights, axis=2) * lag_values[None, :], axis=1)
    shift_cols = jnp.sum(jnp.sum(weights, axis=1) * lag_values[None, :], axis=1)
    return jnp.stack([shift_rows, shift_cols])


def pad_axis(values, before, after, axis_pos):
    widths = [(0, 0)] * values.ndim
    widths[axis_pos % values.ndim] = (before, after)
    return jnp.pad(values, widths)


def plane_force(field_vals, stiffness, grid_rows):
    full_shape = field_vals.shape
    grid_cols = full_shape[-1] // grid_rows
    grid = field_vals.reshape(full_shape[:-1] + (grid_rows, grid_cols))
    stiff_grid = stiffness.reshape(stiffness.shape[:-1] + (1, grid_rows, grid_cols))
    along_cols = 0.5 * (stiff_grid[..., 1:] + stiff_grid[..., :-1]) * (grid[..., 1:] - grid[..., :-1])
    col_force = pad_axis(along_cols, 1, 0, -1) - pad_axis(along_cols, 0, 1, -1)
    along_rows = 0.5 * (stiff_grid[..., 1:, :] + stiff_grid[..., :-1, :]) * (grid[..., 1:, :] - grid[..., :-1, :])
    row_force = pad_axis(along_rows, 1, 0, -2) - pad_axis(along_rows, 0, 1, -2)
    return (col_force + row_force).reshape(full_shape)


def mesh_force(middle, upper, lower, here_field, below_field, stiffness, grid_rows):
    gap_here = upper - middle - here_field[..., 0:2, :]
    gap_below = middle - lower - below_field[..., 0:2, :]
    return plane_force(middle, stiffness, grid_rows) - here_field[..., 2:3, :] * gap_here + below_field[..., 2:3, :] * gap_below


def shift_up(values):
    return jnp.concatenate([values[1:], jnp.zeros_like(values[:1])], axis=0)


def shift_down(values):
    return jnp.concatenate([jnp.zeros_like(values[:1]), values[:-1]], axis=0)


def reference(patches, pair_list, pair_count, tissue):
    cosine_table, sine_table = dft_tables(PS)
    above_all = shift_up(patches)

    def per_section(section_items):
        own_patches, next_patches, listing, live_count = section_items
        valid_mask = (jnp.arange(LIST) < live_count).astype(jnp.float32)
        slot_flows = soft_peak(own_patches[listing], next_patches[listing], cosine_table, sine_table) * valid_mask[None, :]
        onehot = (listing[:, None] == jnp.arange(P_SIZE)[None, :]).astype(jnp.float32) * valid_mask[:, None]
        moved_flows = jnp.dot(slot_flows, onehot, precision=lax.Precision.HIGHEST)
        pair_field = jnp.concatenate([moved_flows, jnp.sum(onehot, axis=0)[None, :]], axis=0)
        return slot_flows, pair_field

    pair_flow, pair_field = lax.map(per_section, (patches, above_all, pair_list, pair_count))
    stiffness = spring_rate * (1.0 + 2.0 * tissue.astype(jnp.float32))
    positions = jnp.zeros((SEC, 2, P_SIZE), jnp.float32)
    below_field = shift_down(pair_field)
    for sweep_step in range(ITERS):
        force_now = mesh_force(positions, shift_up(positions), shift_down(positions), pair_field, below_field, stiffness, GR)
        positions = positions - step_rate * force_now
    return pair_flow, positions
```

```python
import functools

import jax
import jax.numpy as jnp
import numpy as np
from jax import lax
from jax.experimental import pallas as pl
from jax.experimental.pallas import tpu as pltpu
from jax.sharding import PartitionSpec as P

GR = 8
SPRING = 0.25
STEP = 0.15
CHUNK = 8
PIECE = 2
LOADS = 4
HALO = 3
MESH = pl.DeviceIdType.MESH
F32 = jnp.float32
BF16 = jnp.bfloat16


def dft_tables(length):
    index = np.arange(length)
    angle = (index[:, None] * index[None, :] % length) * (2.0 * np.pi / length)
    c = np.cos(angle).astype(np.float32)
    s = np.sin(angle).astype(np.float32)
    right = np.concatenate([c, s], axis=1)
    left = np.block([[c, -s], [-s, -c]])
    inner = np.block([[c, s], [-s, c]])
    last = np.concatenate([c, -s], axis=1)
    tables = np.concatenate([right, left, inner, last], axis=0)
    return jnp.asarray(tables.astype(jnp.bfloat16))


def dot(a, b):
    return jnp.dot(a, b, preferred_element_type=F32)


def dot_nt(a, b):
    return lax.dot_general(a, b, (((1,), (1,)), ((), ())), preferred_element_type=F32)


def split3(x):
    top = x.astype(BF16)
    rest = x - top.astype(F32)
    mid = rest.astype(BF16)
    return top, mid, (rest - mid.astype(F32)).astype(BF16)


def stacked(both, a, b, side):
    ra = both[a * side : (a + 1) * side]
    rb = both[b * side : (b + 1) * side]
    top = jnp.concatenate([ra[:, :side], rb[:, :side]], axis=1)
    low = jnp.concatenate([ra[:, side:], rb[:, side:]], axis=1)
    return jnp.concatenate([top, low], axis=0)


def spectra(images, right, left):
    side = images[0].shape[0]
    rows = jnp.concatenate(images, axis=0)
    both = dot(rows, right).astype(BF16)
    return [dot(left, stacked(both, 2 * i, 2 * i + 1, side)) for i in range(len(images) // 2)]


def lane_roll(x, shift):
    return pltpu.roll(x, shift % x.shape[-1], x.ndim - 1)


def single(pair):
    return pair % 2


def up_chunks(pair, n, chunks):
    return chunks * ((pair + 1) // 2) // (n // 2)


def exchange(
    n,
    tables_any,
    list_any,
    count_s,
    tissue_any,
    patches_any,
    out_ref,
    patches,
    tables,
    list_v,
    list_s,
    tissue_v,
    note,
    far_note,
    far_s,
    outgoing,
    incoming,
    own_spec,
    peak_ref,
    mass_ref,
    moment_ref,
    packet,
    halo,
    load_sems,
    smem_sem,
    list_sems,
    send_sems,
    recv_sems,
    halo_send,
    halo_recv,
):
    me = lax.axis_index("sec")
    total, side, _ = patches.shape
    slots = list_v.shape[1]
    chunks = slots // CHUNK
    offsets = [d for d in range(-HALO, HALO + 1) if d != 0]

    loads = [
        pltpu.make_async_copy(source, target, load_sems.at[i])
        for i, (source, target) in enumerate(
            (
                (list_any, list_s),
                (list_any, list_v),
                (patches_any.at[0], patches),
                (tables_any, tables),
                (tissue_any, tissue_v),
            )
        )
    ]
    loads[0].start()
    loads[1].start()
    part = total // LOADS
    for i in range(LOADS):
        rows = pl.ds(i * part, part)
        pltpu.make_async_copy(patches_any.at[0, rows], patches.at[rows], load_sems.at[2]).start()
    loads[3].start()
    loads[4].start()

    halo[...] = jnp.zeros_like(halo)
    far_note[...] = jnp.zeros_like(far_note)

    barrier = pltpu.get_barrier_semaphore()
    for d in offsets:

        @pl.when((me + d >= 0) & (me + d < n))
        def _():
            pl.semaphore_signal(barrier, inc=1, device_id={"sec": me + d}, device_id_type=MESH)

    peak_ref[...] = jnp.zeros_like(peak_ref)
    mass_ref[...] = jnp.ones_like(mass_ref)
    moment_ref[...] = jnp.zeros_like(moment_ref)
    loads[0].wait()
    loads[1].wait()
    count = count_s[0]
    note[...] = jnp.concatenate([list_v[...], jnp.full((1, slots), count, jnp.int32)], axis=0)

    has_up = jnp.minimum(n - 1 - me, 1)
    has_down = jnp.minimum(me, 1)
    my_up = up_chunks(me, n, chunks)
    far_up = up_chunks(me - 1, n, chunks)
    my_half = has_up * single(me)
    far_half = has_down * single(me - 1)

    pl.semaphore_wait(barrier, jnp.minimum(me, HALO) + jnp.minimum(n - 1 - me, HALO))

    list_copy = pltpu.make_async_remote_copy(
        src_ref=note,
        dst_ref=far_note,
        send_sem=list_sems.at[0],
        recv_sem=list_sems.at[1],
        device_id={"sec": me + 1},
        device_id_type=MESH,
    )

    @pl.when(me < n - 1)
    def _():
        list_copy.start()

    loads[2].wait()

    def patch_copy(q, to):
        return pltpu.make_async_remote_copy(
            src_ref=outgoing.at[pl.ds(q * CHUNK, CHUNK)],
            dst_ref=incoming.at[pl.ds(q * CHUNK, CHUNK)],
            send_sem=send_sems.at[q],
            recv_sem=recv_sems.at[q],
            device_id={"sec": to},
            device_id_type=MESH,
        )

    def piece_copy(q, first, size, to):
        at = pl.ds(q * CHUNK + first, size)
        return pltpu.make_async_remote_copy(
            src_ref=outgoing.at[at],
            dst_ref=incoming.at[at],
            send_sem=send_sems.at[q],
            recv_sem=recv_sems.at[q],
            device_id={"sec": to},
            device_id_type=MESH,
        )

    def gather(source, q, c, first, count):
        for j in range(first, first + count):
            outgoing[q * CHUNK + j] = patches[source[0, c * CHUNK + j]]

    def send_up(c, carry):
        gather(list_s, c, c, 0, CHUNK)
        patch_copy(c, me + 1).start()
        return carry

    lax.fori_loop(0, has_up * my_up, send_up, 0)

    @pl.when(my_half > 0)
    def _():
        gather(list_s, my_up, my_up, 0, PIECE)
        piece_copy(my_up, 0, PIECE, me + 1).start()

    right_ref = tables.at[0:side]
    left_ref = tables.at[side : 3 * side]
    inner_ref = tables.at[3 * side : 5 * side]
    last_ref = tables.at[5 * side : 6 * side]

    def own_group(q, carry):
        images = []
        for j in range(CHUNK):
            far = far_s[0, jnp.minimum(q, chunks - 1) * CHUNK + j]
            near = list_s[0, jnp.maximum(q - chunks, 0) * CHUNK + j]
            images.append(patches[jnp.where(q < chunks, far, near)])
        for i, spec in enumerate(spectra(images, right_ref[...], left_ref[...])):
            own_spec[q * (CHUNK // 2) + i] = spec.astype(BF16)
        return carry

    @pl.when(me > 0)
    def _():
        list_copy.wait_recv()

    to_smem = pltpu.make_async_copy(far_note, far_s, smem_sem)
    to_smem.start()
    to_smem.wait()

    @pl.when(far_half > 0)
    def _():
        gather(far_s, chunks + far_up, far_up, PIECE, CHUNK - PIECE)
        piece_copy(chunks + far_up, PIECE, CHUNK - PIECE, me - 1).start()

    down_from = far_up + far_half

    def send_down(c, carry):
        gather(far_s, chunks + c, c, 0, CHUNK)
        patch_copy(chunks + c, me - 1).start()
        return carry

    lax.fori_loop(down_from, down_from + has_down * (chunks - down_from), send_down, 0)
    for load in loads[3:]:
        load.wait()
    lax.fori_loop(chunks + my_up, chunks + my_up + has_up * (chunks - my_up), own_group, 0)
    lax.fori_loop(0, has_down * far_up + far_half, own_group, 0)

    half = side // 2
    row = lax.broadcasted_iota(jnp.int32, (side, 1), 0)
    row_lag = ((row + half) % side - half).astype(F32)
    scale = 64.0 / float(side * side * side * side)

    def match_group(t, carry):
        start_a, count_a, start_b = carry
        q = jnp.where(t < count_a, start_a + t, start_b + t - count_a)
        is_far_half = (q == far_up) & (far_half > 0)
        is_my_half = (q == chunks + my_up) & (my_half > 0)

        @pl.when(is_far_half)
        def _():
            piece_copy(q, 0, PIECE, me).wait_recv()

        @pl.when(is_my_half)
        def _():
            piece_copy(q, PIECE, CHUNK - PIECE, me).wait_recv()

        @pl.when(jnp.logical_not(is_far_half | is_my_half))
        def _():
            patch_copy(q, me).wait_recv()

        sign = jnp.where(q < chunks, -1.0, 1.0).astype(F32)
        images = [incoming[q * CHUNK + j] for j in range(CHUNK)]
        crosses = []
        for i, spec in enumerate(spectra(images, right_ref[...], left_ref[...])):
            ar = spec[:side].astype(BF16).astype(F32)
            ai = spec[side:].astype(BF16).astype(F32)
            own = own_spec[q * (CHUNK // 2) + i].astype(F32)
            br, bi = own[:side], own[side:]
            cr = (br * ar + bi * ai).astype(BF16)
            ci = ((br * ai - bi * ar) * sign).astype(BF16)
            crosses.append(jnp.concatenate([cr[:, :side], ci[:, :side]], axis=1))
            crosses.append(jnp.concatenate([cr[:, side:], ci[:, side:]], axis=1))
        inner = dot(jnp.concatenate(crosses, axis=0), inner_ref[...]).astype(BF16)
        peaks, masses, moments = [], [], []
        for i in range(CHUNK // 2):
            scores = dot(last_ref[...], stacked(inner, 2 * i, 2 * i + 1, side)) * scale
            peak = jnp.max(scores, axis=0, keepdims=True)
            e = jnp.exp(scores - peak)
            mass = jnp.sum(e, axis=0, keepdims=True)
            moment = jnp.sum(e * row_lag, axis=0, keepdims=True)
            for parts, value in ((peaks, peak), (masses, mass), (moments, moment)):
                parts.append(value[:, :side])
                parts.append(value[:, side:])
        at = pl.ds(pl.multiple_of(q * CHUNK, CHUNK), CHUNK)
        peak_ref[at, :] = jnp.concatenate(peaks, axis=0)
        mass_ref[at, :] = jnp.concatenate(masses, axis=0)
        moment_ref[at, :] = jnp.concatenate(moments, axis=0)
        return carry

    n_far = has_down * far_up + far_half
    n_near = has_up * (chunks - my_up)
    odd = me % 2
    start_a = (1 - odd) * (chunks + my_up)
    start_b = odd * (chunks + my_up)
    count_a = odd * n_far + (1 - odd) * n_near
    lax.fori_loop(0, n_far + n_near, match_group, (start_a, count_a, start_b))

    peak = peak_ref[...]
    weight = jnp.exp(peak - jnp.max(peak, axis=1, keepdims=True))
    mass = mass_ref[...] * weight
    moment = moment_ref[...] * weight
    col = lax.broadcasted_iota(jnp.int32, (8, side), 1)
    sub = lax.broadcasted_iota(jnp.int32, (8, side), 0)
    col_lag = ((col + half) % side - half).astype(F32)
    axes = jnp.where(sub == 0, 1.0, jnp.where(sub == 1, col_lag, 0.0))
    thirds = jnp.concatenate(split3(jnp.concatenate([mass, moment], axis=0)), axis=0)
    triple = dot_nt(axes.astype(BF16), thirds)
    span = 4 * slots
    joined = triple[:, 0:span] + triple[:, span : 2 * span] + triple[:, 2 * span :]
    sums, rows_num = joined[:, 0 : 2 * slots], joined[:, 2 * slots :]
    mass_all = sums[0:1]
    place = lax.broadcasted_iota(jnp.int32, (1, 2 * slots), 1)
    is_far = place < slots
    far = far_note[...]
    counts = jnp.concatenate([far[1:2], jnp.full((1, slots), count, jnp.int32)], axis=1)
    lists = jnp.concatenate([far[0:1], list_v[...]], axis=1)
    slot = jnp.where(is_far, place, place - slots)
    first = jnp.where(is_far, 0, (chunks - n_near) * CHUNK + my_half * PIECE)
    stop = jnp.minimum(jnp.where(is_far, n_far * CHUNK - far_half * (CHUNK - PIECE), slots), counts)
    live = (slot >= first) & (slot < stop)
    flow_rows = jnp.where(live, rows_num[0:1] / mass_all, 0.0)
    flow_cols = jnp.where(live, sums[1:2] / mass_all, 0.0)
    which = lax.broadcasted_iota(jnp.int32, (total, 2 * slots), 0)
    onehot = (which == lists).astype(F32).astype(BF16)
    one_pair = jnp.concatenate(
        [flow_rows, flow_cols, live.astype(F32), jnp.zeros((5, 2 * slots), F32)], axis=0
    )
    both = jnp.concatenate(
        [jnp.where(is_far, one_pair, 0.0), jnp.where(is_far, 0.0, one_pair)], axis=0
    )
    triple = dot_nt(jnp.concatenate(split3(both), axis=0), onehot)
    field = triple[0:16] + triple[16:32] + triple[32:48]
    packet[0:3] = field[0:3]
    packet[3:4] = tissue_v[...].astype(F32)
    packet[4:8] = field[4:8]
    packet[8:16] = field[8:16]
    packet[4:5, 0 : 2 * slots] = flow_rows
    packet[5:6, 0 : 2 * slots] = flow_cols

    def halo_copy(d):
        return pltpu.make_async_remote_copy(
            src_ref=packet,
            dst_ref=halo.at[HALO - d],
            send_sem=halo_send.at[HALO - d],
            recv_sem=halo_recv.at[HALO - d],
            device_id={"sec": me + d},
            device_id_type=MESH,
        )

    for d in offsets:

        @pl.when((me + d >= 0) & (me + d < n))
        def _():
            halo_copy(d).start()

    @pl.when(me < n - 1)
    def _():
        list_copy.wait_send()

    def drain_up(c, carry):
        patch_copy(c, me + 1).wait_send()
        return carry

    lax.fori_loop(0, has_up * my_up, drain_up, 0)

    @pl.when(my_half > 0)
    def _():
        piece_copy(my_up, 0, PIECE, me + 1).wait_send()

    def drain_down(c, carry):
        patch_copy(chunks + c, me - 1).wait_send()
        return carry

    lax.fori_loop(down_from, down_from + has_down * (chunks - down_from), drain_down, 0)

    @pl.when(far_half > 0)
    def _():
        piece_copy(chunks + far_up, PIECE, CHUNK - PIECE, me - 1).wait_send()

    for d in offsets:

        @pl.when((me - d >= 0) & (me - d < n))
        def _():
            halo_copy(d).wait_recv()

    halo[HALO] = packet[...]
    relax(slots, halo, out_ref)
    for d in offsets:

        @pl.when((me + d >= 0) & (me + d < n))
        def _():
            halo_copy(d).wait_send()


def relax(slots, halo, out_ref):
    total = halo.shape[-1]
    near, above = halo[HALO], halo[HALO + 1]
    out_ref[2:4, 0:slots] = near[4:6, slots : 2 * slots] + above[4:6, 0:slots]
    fields = {d: halo[HALO + d][8:16] + halo[HALO + d + 1][0:8] for d in range(-HALO, HALO)}
    links = {d: jnp.broadcast_to(f[2:3], f.shape) for d, f in fields.items()}
    lane = lax.broadcasted_iota(jnp.int32, (8, total), 1)
    width = total // GR
    has_right = (lane % width) != width - 1
    has_below = lane < total - width

    def springs(d):
        tissue = jnp.broadcast_to(halo[HALO + d][3:4], (8, total))
        stiff = SPRING * (1.0 + 2.0 * tissue)
        across = jnp.where(has_right, 0.5 * (stiff + lane_roll(stiff, -1)), 0.0)
        along = jnp.where(has_below, 0.5 * (stiff + lane_roll(stiff, -width)), 0.0)
        return across, along

    def plane(u, spring):
        across, along = spring
        a = across * (lane_roll(u, -1) - u)
        b = along * (lane_roll(u, -width) - u)
        return (lane_roll(a, 1) - a) + (lane_roll(b, width) - b)

    spring = {d: springs(d) for d in (-1, 0, 1)}
    pull = {d: links[d] * fields[d] for d in fields}
    u1 = {d: -STEP * (pull[d] - pull[d - 1]) for d in range(-2, 3)}

    def relaxed(u, d):
        gap_here = u[d + 1] - u[d] - fields[d]
        gap_below = u[d] - u[d - 1] - fields[d - 1]
        force = plane(u[d], spring[d]) - links[d] * gap_here + links[d - 1] * gap_below
        return u[d] - STEP * force

    u2 = {d: relaxed(u1, d) for d in (-1, 0, 1)}
    out_ref[0:2] = relaxed(u2, 0)[0:2]


def unpack(both, flow_ref, pos_ref):
    flow_ref[0] = both[2:4, 0 : flow_ref.shape[-1]]
    pos_ref[0] = both[0:2]


def on_device(n, patches, pair_list, pair_count, tissue):
    _, total, side, _ = patches.shape
    slots = pair_list.shape[1]
    chunks = slots // CHUNK
    vmem = pl.BlockSpec(memory_space=pltpu.VMEM)
    any_space = pl.BlockSpec(memory_space=pl.ANY)
    dma = pltpu.SemaphoreType.DMA
    both = pl.pallas_call(
        functools.partial(exchange, n),
        out_shape=pltpu.VMEM((4, total), F32),
        in_specs=[any_space] * 2 + [pl.BlockSpec(memory_space=pltpu.SMEM)] + [any_space] * 2,
        out_specs=vmem,
        scratch_shapes=[
            pltpu.VMEM((total, side, side), BF16),
            pltpu.VMEM((6 * side, 2 * side), BF16),
            pltpu.VMEM((1, slots), jnp.int32),
            pltpu.SMEM((1, slots), jnp.int32),
            pltpu.VMEM((1, total), jnp.int32),
            pltpu.VMEM((2, slots), jnp.int32),
            pltpu.VMEM((2, slots), jnp.int32),
            pltpu.SMEM((2, slots), jnp.int32),
            pltpu.VMEM((2 * slots, side, side), BF16),
            pltpu.VMEM((2 * slots, side, side), BF16),
            pltpu.VMEM((slots, 2 * side, 2 * side), BF16),
            pltpu.VMEM((2 * slots, side), F32),
            pltpu.VMEM((2 * slots, side), F32),
            pltpu.VMEM((2 * slots, side), F32),
            pltpu.VMEM((16, total), F32),
            pltpu.VMEM((2 * HALO + 1, 16, total), F32),
            dma((5,)),
            dma,
            dma((2,)),
            dma((2 * chunks,)),
            dma((2 * chunks,)),
            dma((2 * HALO + 1,)),
            dma((2 * HALO + 1,)),
        ],
        compiler_params=pltpu.CompilerParams(
            collective_id=0, has_side_effects=True, vmem_limit_bytes=64_000_000
        ),
        name="exchange",
    )(dft_tables(side), pair_list, pair_count, tissue, patches)
    return pl.pallas_call(
        unpack,
        out_shape=(
            jax.ShapeDtypeStruct((1, 2, slots), F32),
            jax.ShapeDtypeStruct((1, 2, total), F32),
        ),
        in_specs=[vmem],
        out_specs=(vmem, vmem),
        compiler_params=pltpu.CompilerParams(vmem_limit_bytes=2_000_000),
        name="unpack",
    )(both)


def solution(mesh):
    return jax.shard_map(
        functools.partial(on_device, mesh.shape["sec"]),
        mesh=mesh,
        in_specs=(
            P(("group", "sec"), None, None, None),
            P(("group", "sec"), None),
            P(("group", "sec")),
            P(("group", "sec"), None),
        ),
        out_specs=(P(("group", "sec"), None, None), P(("group", "sec"), None, None)),
        check_vma=False,
    )
```

```python
import functools

import jax
import jax.numpy as jnp
import numpy as np
from jax import lax
from jax.experimental import pallas as pl
from jax.experimental.pallas import tpu as pltpu
from jax.sharding import PartitionSpec as P

GR = 8
SPRING = 0.25
STEP = 0.15
CHUNK = 8
PIECE = 2
BANDS = 2
HALO = 3
MESH = pl.DeviceIdType.MESH
F32 = jnp.float32
BF16 = jnp.bfloat16


def dft_tables(length):
    index = np.arange(length)
    angle = (index[:, None] * index[None, :] % length) * (2.0 * np.pi / length)
    c = np.cos(angle).astype(np.float32)
    s = np.sin(angle).astype(np.float32)
    right = np.concatenate([c, s], axis=1)
    left = np.block([[c, -s], [-s, -c]])
    inner = np.block([[c, s], [-s, c]])
    last = np.concatenate([c, -s], axis=1)
    tables = np.concatenate([right, left, inner, last], axis=0)
    return jnp.asarray(tables.astype(jnp.bfloat16))


def dot(a, b):
    return jnp.dot(a, b, preferred_element_type=F32)


def dot_nt(a, b):
    return lax.dot_general(a, b, (((1,), (1,)), ((), ())), preferred_element_type=F32)


def split3(x):
    top = x.astype(BF16)
    rest = x - top.astype(F32)
    mid = rest.astype(BF16)
    return top, mid, (rest - mid.astype(F32)).astype(BF16)


def stacked(both, a, b, side):
    ra = both[a * side : (a + 1) * side]
    rb = both[b * side : (b + 1) * side]
    top = jnp.concatenate([ra[:, :side], rb[:, :side]], axis=1)
    low = jnp.concatenate([ra[:, side:], rb[:, side:]], axis=1)
    return jnp.concatenate([top, low], axis=0)


def spectra(images, right, left):
    side = images[0].shape[0]
    rows = jnp.concatenate(images, axis=0)
    both = dot(rows, right).astype(BF16)
    return [dot(left, stacked(both, 2 * i, 2 * i + 1, side)) for i in range(len(images) // 2)]


def lane_roll(x, shift):
    return pltpu.roll(x, shift % x.shape[-1], x.ndim - 1)


def single(pair):
    return pair % 2


def up_chunks(pair, n, chunks):
    return chunks * ((pair + 1) // 2) // (n // 2)


def exchange(
    n,
    tables_any,
    list_any,
    count_s,
    tissue_any,
    patches_any,
    out_ref,
    patches_a,
    patches_b,
    tables,
    list_v,
    list_s,
    tissue_v,
    note,
    far_note,
    far_s,
    outgoing,
    incoming,
    own_spec,
    peak_ref,
    mass_ref,
    moment_ref,
    packet,
    halo,
    load_sems,
    list_sems,
    send_sems,
    recv_sems,
    halo_send,
    halo_recv,
    near_sem,
    far_sem,
):
    me = lax.axis_index("sec")
    patches = (patches_a, patches_b)
    total, _, side = patches_a.shape
    slots = list_v.shape[1]
    chunks = slots // CHUNK
    offsets = [d for d in range(-HALO, HALO + 1) if d != 0]

    loads = [
        pltpu.make_async_copy(source, target, load_sems.at[i])
        for i, (source, target) in enumerate(
            (
                (list_any, list_s),
                (list_any, list_v),
                (tables_any, tables),
                (tissue_any, tissue_v),
            )
        )
    ]
    loads[0].start()
    loads[1].start()
    bands = [pl.ds(i * side // BANDS, side // BANDS) for i in range(BANDS)]
    band_loads = [
        pltpu.make_async_copy(
            patches_any.at[0, :, band], patches[i], load_sems.at[4 + i]
        )
        for i, band in enumerate(bands)
    ]
    for load in band_loads:
        load.start()
    loads[2].start()
    loads[3].start()

    halo[...] = jnp.zeros_like(halo)
    far_note[...] = jnp.zeros_like(far_note)

    barrier = pltpu.get_barrier_semaphore()

    def greet(sem):
        for to in (me + 1 - 2 * (me % 2), me - 1 + 2 * (me % 2)):

            @pl.when((to >= 0) & (to < n))
            def _():
                pl.semaphore_signal(sem, inc=1, device_id={"sec": to}, device_id_type=MESH)

    greet(barrier)

    peak_ref[...] = jnp.zeros_like(peak_ref)
    mass_ref[...] = jnp.ones_like(mass_ref)
    moment_ref[...] = jnp.zeros_like(moment_ref)
    loads[0].wait()
    loads[1].wait()
    count = count_s[0]
    note[...] = jnp.concatenate([list_v[...], jnp.full((1, slots), count, jnp.int32)], axis=0)

    has_up = jnp.minimum(n - 1 - me, 1)
    has_down = jnp.minimum(me, 1)
    my_up = up_chunks(me, n, chunks)
    far_up = up_chunks(me - 1, n, chunks)
    my_half = has_up * single(me)
    far_half = has_down * single(me - 1)

    sides = jnp.minimum(me, 1) + jnp.minimum(n - 1 - me, 1)
    pl.semaphore_wait(barrier, sides)

    list_copy = pltpu.make_async_remote_copy(
        src_ref=note,
        dst_ref=far_note,
        send_sem=list_sems.at[0],
        recv_sem=list_sems.at[1],
        device_id={"sec": me + 1},
        device_id_type=MESH,
    )

    slot_copy = pltpu.make_async_remote_copy(
        src_ref=list_v,
        dst_ref=far_s,
        send_sem=list_sems.at[2],
        recv_sem=list_sems.at[3],
        device_id={"sec": me + 1},
        device_id_type=MESH,
    )

    @pl.when(me < n - 1)
    def _():
        slot_copy.start()
        list_copy.start()


    def patch_copy(q, to):
        return pltpu.make_async_remote_copy(
            src_ref=outgoing.at[pl.ds(q * CHUNK, CHUNK)],
            dst_ref=incoming.at[pl.ds(q * CHUNK, CHUNK)],
            send_sem=send_sems.at[q],
            recv_sem=recv_sems.at[q],
            device_id={"sec": to},
            device_id_type=MESH,
        )

    def piece_copy(q, first, size, to):
        at = pl.ds(q * CHUNK + first, size)
        return pltpu.make_async_remote_copy(
            src_ref=outgoing.at[at],
            dst_ref=incoming.at[at],
            send_sem=send_sems.at[q],
            recv_sem=recv_sems.at[q],
            device_id={"sec": to},
            device_id_type=MESH,
        )

    def gather(source, q, c, first, count):
        for j in range(first, first + count):
            for part, band in zip(patches, bands):
                outgoing[q * CHUNK + j, band] = part[source[0, c * CHUNK + j]]

    def send_up(c, carry):
        gather(list_s, c, c, 0, CHUNK)
        patch_copy(c, me + 1).start()
        return carry

    for i, band in enumerate(bands):
        band_loads[i].wait()

        @pl.when(has_up * my_up > 0)
        def _():
            for j in range(CHUNK):
                outgoing[j, band] = patches[i][list_s[0, j]]
            pltpu.make_async_remote_copy(
                src_ref=outgoing.at[0:CHUNK, band],
                dst_ref=incoming.at[0:CHUNK, band],
                send_sem=send_sems.at[0],
                recv_sem=recv_sems.at[0],
                device_id={"sec": me + 1},
                device_id_type=MESH,
            ).start()

    lax.fori_loop(1, has_up * my_up, send_up, 0)

    @pl.when(my_half > 0)
    def _():
        gather(list_s, my_up, my_up, 0, PIECE)
        piece_copy(my_up, 0, PIECE, me + 1).start()

    greet(near_sem)
    right_ref = tables.at[0:side]
    left_ref = tables.at[side : 3 * side]
    inner_ref = tables.at[3 * side : 5 * side]
    last_ref = tables.at[5 * side : 6 * side]

    def own_group(q, carry):
        images = []
        for j in range(CHUNK):
            far = far_s[0, jnp.minimum(q, chunks - 1) * CHUNK + j]
            near = list_s[0, jnp.maximum(q - chunks, 0) * CHUNK + j]
            at = jnp.where(q < chunks, far, near)
            images.append(jnp.concatenate([part[at] for part in patches], axis=0))
        for i, spec in enumerate(spectra(images, right_ref[...], left_ref[...])):
            own_spec[q * (CHUNK // 2) + i] = spec.astype(BF16)
        return carry

    @pl.when(me > 0)
    def _():
        slot_copy.wait_recv()

    @pl.when(me == 0)
    def _():
        fill = pltpu.make_async_copy(list_v, far_s, list_sems.at[3])
        fill.start()
        fill.wait()

    @pl.when(far_half > 0)
    def _():
        gather(far_s, chunks + far_up, far_up, PIECE, CHUNK - PIECE)
        piece_copy(chunks + far_up, PIECE, CHUNK - PIECE, me - 1).start()

    down_from = far_up + far_half

    def send_down(c, carry):
        gather(far_s, chunks + c, c, 0, CHUNK)
        patch_copy(chunks + c, me - 1).start()
        return carry

    lax.fori_loop(down_from, down_from + has_down * (chunks - down_from), send_down, 0)
    for load in loads[2:]:
        load.wait()
    lax.fori_loop(chunks + my_up, chunks + my_up + has_up * (chunks - my_up), own_group, 0)
    lax.fori_loop(0, has_down * far_up + far_half, own_group, 0)

    pl.semaphore_wait(near_sem, sides)
    greet(far_sem)
    @pl.when(me > 0)
    def _():
        list_copy.wait_recv()

    half = side // 2
    row = lax.broadcasted_iota(jnp.int32, (side, 1), 0)
    row_lag = ((row + half) % side - half).astype(F32)
    scale = 64.0 / float(side * side * side * side)

    def match_group(t, carry):
        start_a, count_a, start_b = carry
        q = jnp.where(t < count_a, start_a + t, start_b + t - count_a)
        is_far_half = (q == far_up) & (far_half > 0)
        is_my_half = (q == chunks + my_up) & (my_half > 0)

        @pl.when(is_far_half)
        def _():
            piece_copy(q, 0, PIECE, me).wait_recv()

        @pl.when(is_my_half)
        def _():
            piece_copy(q, PIECE, CHUNK - PIECE, me).wait_recv()

        @pl.when(jnp.logical_not(is_far_half | is_my_half))
        def _():
            patch_copy(q, me).wait_recv()

        sign = jnp.where(q < chunks, -1.0, 1.0).astype(F32)
        images = [incoming[q * CHUNK + j] for j in range(CHUNK)]
        crosses = []
        for i, spec in enumerate(spectra(images, right_ref[...], left_ref[...])):
            ar = spec[:side].astype(BF16).astype(F32)
            ai = spec[side:].astype(BF16).astype(F32)
            own = own_spec[q * (CHUNK // 2) + i].astype(F32)
            br, bi = own[:side], own[side:]
            cr = (br * ar + bi * ai).astype(BF16)
            ci = ((br * ai - bi * ar) * sign).astype(BF16)
            crosses.append(jnp.concatenate([cr[:, :side], ci[:, :side]], axis=1))
            crosses.append(jnp.concatenate([cr[:, side:], ci[:, side:]], axis=1))
        inner = dot(jnp.concatenate(crosses, axis=0), inner_ref[...]).astype(BF16)
        peaks, masses, moments = [], [], []
        for i in range(CHUNK // 2):
            scores = dot(last_ref[...], stacked(inner, 2 * i, 2 * i + 1, side)) * scale
            peak = jnp.max(scores, axis=0, keepdims=True)
            e = jnp.exp(scores - peak)
            mass = jnp.sum(e, axis=0, keepdims=True)
            moment = jnp.sum(e * row_lag, axis=0, keepdims=True)
            for parts, value in ((peaks, peak), (masses, mass), (moments, moment)):
                parts.append(value[:, :side])
                parts.append(value[:, side:])
        at = pl.ds(pl.multiple_of(q * CHUNK, CHUNK), CHUNK)
        peak_ref[at, :] = jnp.concatenate(peaks, axis=0)
        mass_ref[at, :] = jnp.concatenate(masses, axis=0)
        moment_ref[at, :] = jnp.concatenate(moments, axis=0)
        return carry

    n_far = has_down * far_up + far_half
    n_near = has_up * (chunks - my_up)
    odd = me % 2
    start_a = (1 - odd) * (chunks + my_up)
    start_b = odd * (chunks + my_up)
    count_a = odd * n_far + (1 - odd) * n_near
    lax.fori_loop(0, n_far + n_near, match_group, (start_a, count_a, start_b))

    peak = peak_ref[...]
    weight = jnp.exp(peak - jnp.max(peak, axis=1, keepdims=True))
    mass = mass_ref[...] * weight
    moment = moment_ref[...] * weight
    col = lax.broadcasted_iota(jnp.int32, (8, side), 1)
    sub = lax.broadcasted_iota(jnp.int32, (8, side), 0)
    col_lag = ((col + half) % side - half).astype(F32)
    axes = jnp.where(sub == 0, 1.0, jnp.where(sub == 1, col_lag, 0.0))
    thirds = jnp.concatenate(split3(jnp.concatenate([mass, moment], axis=0)), axis=0)
    triple = dot_nt(axes.astype(BF16), thirds)
    span = 4 * slots
    joined = triple[:, 0:span] + triple[:, span : 2 * span] + triple[:, 2 * span :]
    sums, rows_num = joined[:, 0 : 2 * slots], joined[:, 2 * slots :]
    mass_all = sums[0:1]
    place = lax.broadcasted_iota(jnp.int32, (1, 2 * slots), 1)
    is_far = place < slots
    far = far_note[...]
    counts = jnp.concatenate([far[1:2], jnp.full((1, slots), count, jnp.int32)], axis=1)
    lists = jnp.concatenate([far[0:1], list_v[...]], axis=1)
    slot = jnp.where(is_far, place, place - slots)
    first = jnp.where(is_far, 0, (chunks - n_near) * CHUNK + my_half * PIECE)
    stop = jnp.minimum(jnp.where(is_far, n_far * CHUNK - far_half * (CHUNK - PIECE), slots), counts)
    live = (slot >= first) & (slot < stop)
    flow_rows = jnp.where(live, rows_num[0:1] / mass_all, 0.0)
    flow_cols = jnp.where(live, sums[1:2] / mass_all, 0.0)
    which = lax.broadcasted_iota(jnp.int32, (total, 2 * slots), 0)
    onehot = (which == lists).astype(F32).astype(BF16)
    one_pair = jnp.concatenate(
        [flow_rows, flow_cols, live.astype(F32), jnp.zeros((5, 2 * slots), F32)], axis=0
    )
    both = jnp.concatenate(
        [jnp.where(is_far, one_pair, 0.0), jnp.where(is_far, 0.0, one_pair)], axis=0
    )
    triple = dot_nt(jnp.concatenate(split3(both), axis=0), onehot)
    field = triple[0:16] + triple[16:32] + triple[32:48]
    packet[0:3] = field[0:3]
    packet[3:4] = tissue_v[...].astype(F32)
    packet[4:8] = field[4:8]
    packet[8:16] = field[8:16]
    packet[4:5, 0 : 2 * slots] = flow_rows
    packet[5:6, 0 : 2 * slots] = flow_cols

    pl.semaphore_wait(far_sem, sides)

    def halo_copy(d):
        return pltpu.make_async_remote_copy(
            src_ref=packet,
            dst_ref=halo.at[HALO - d],
            send_sem=halo_send.at[HALO - d],
            recv_sem=halo_recv.at[HALO - d],
            device_id={"sec": me + d},
            device_id_type=MESH,
        )

    for d in offsets:

        @pl.when((me + d >= 0) & (me + d < n))
        def _():
            halo_copy(d).start()

    @pl.when(me < n - 1)
    def _():
        slot_copy.wait_send()
        list_copy.wait_send()

    def drain_up(c, carry):
        patch_copy(c, me + 1).wait_send()
        return carry

    lax.fori_loop(0, has_up * my_up, drain_up, 0)

    @pl.when(my_half > 0)
    def _():
        piece_copy(my_up, 0, PIECE, me + 1).wait_send()

    def drain_down(c, carry):
        patch_copy(chunks + c, me - 1).wait_send()
        return carry

    lax.fori_loop(down_from, down_from + has_down * (chunks - down_from), drain_down, 0)

    @pl.when(far_half > 0)
    def _():
        piece_copy(chunks + far_up, PIECE, CHUNK - PIECE, me - 1).wait_send()

    for d in offsets:

        @pl.when((me - d >= 0) & (me - d < n))
        def _():
            halo_copy(d).wait_recv()

    halo[HALO] = packet[...]
    relax(slots, halo, out_ref)
    for d in offsets:

        @pl.when((me + d >= 0) & (me + d < n))
        def _():
            halo_copy(d).wait_send()


def relax(slots, halo, out_ref):
    total = halo.shape[-1]
    near, above = halo[HALO], halo[HALO + 1]
    out_ref[2:4, 0:slots] = near[4:6, slots : 2 * slots] + above[4:6, 0:slots]
    fields = {d: halo[HALO + d][8:16] + halo[HALO + d + 1][0:8] for d in range(-HALO, HALO)}
    links = {d: jnp.broadcast_to(f[2:3], f.shape) for d, f in fields.items()}
    lane = lax.broadcasted_iota(jnp.int32, (8, total), 1)
    width = total // GR
    has_right = (lane % width) != width - 1
    has_below = lane < total - width

    def springs(d):
        tissue = jnp.broadcast_to(halo[HALO + d][3:4], (8, total))
        stiff = SPRING * (1.0 + 2.0 * tissue)
        across = jnp.where(has_right, 0.5 * (stiff + lane_roll(stiff, -1)), 0.0)
        along = jnp.where(has_below, 0.5 * (stiff + lane_roll(stiff, -width)), 0.0)
        return across, along

    def plane(u, spring):
        across, along = spring
        a = across * (lane_roll(u, -1) - u)
        b = along * (lane_roll(u, -width) - u)
        return (lane_roll(a, 1) - a) + (lane_roll(b, width) - b)

    spring = {d: springs(d) for d in (-1, 0, 1)}
    pull = {d: links[d] * fields[d] for d in fields}
    u1 = {d: -STEP * (pull[d] - pull[d - 1]) for d in range(-2, 3)}

    def relaxed(u, d):
        gap_here = u[d + 1] - u[d] - fields[d]
        gap_below = u[d] - u[d - 1] - fields[d - 1]
        force = plane(u[d], spring[d]) - links[d] * gap_here + links[d - 1] * gap_below
        return u[d] - STEP * force

    u2 = {d: relaxed(u1, d) for d in (-1, 0, 1)}
    out_ref[0:2] = relaxed(u2, 0)[0:2]


def unpack(both, flow_ref, pos_ref):
    flow_ref[0] = both[2:4, 0 : flow_ref.shape[-1]]
    pos_ref[0] = both[0:2]


def on_device(n, patches, pair_list, pair_count, tissue):
    _, total, side, _ = patches.shape
    slots = pair_list.shape[1]
    chunks = slots // CHUNK
    vmem = pl.BlockSpec(memory_space=pltpu.VMEM)
    any_space = pl.BlockSpec(memory_space=pl.ANY)
    dma = pltpu.SemaphoreType.DMA
    both = pl.pallas_call(
        functools.partial(exchange, n),
        out_shape=pltpu.VMEM((4, total), F32),
        in_specs=[any_space] * 2 + [pl.BlockSpec(memory_space=pltpu.SMEM)] + [any_space] * 2,
        out_specs=vmem,
        scratch_shapes=[
            pltpu.VMEM((total, side // BANDS, side), BF16),
            pltpu.VMEM((total, side // BANDS, side), BF16),
            pltpu.VMEM((6 * side, 2 * side), BF16),
            pltpu.VMEM((1, slots), jnp.int32),
            pltpu.SMEM((1, slots), jnp.int32),
            pltpu.VMEM((1, total), jnp.int32),
            pltpu.VMEM((2, slots), jnp.int32),
            pltpu.VMEM((2, slots), jnp.int32),
            pltpu.SMEM((1, slots), jnp.int32),
            pltpu.VMEM((2 * slots, side, side), BF16),
            pltpu.VMEM((2 * slots, side, side), BF16),
            pltpu.VMEM((slots, 2 * side, 2 * side), BF16),
            pltpu.VMEM((2 * slots, side), F32),
            pltpu.VMEM((2 * slots, side), F32),
            pltpu.VMEM((2 * slots, side), F32),
            pltpu.VMEM((16, total), F32),
            pltpu.VMEM((2 * HALO + 1, 16, total), F32),
            dma((4 + BANDS,)),
            dma((4,)),
            dma((2 * chunks,)),
            dma((2 * chunks,)),
            dma((2 * HALO + 1,)),
            dma((2 * HALO + 1,)),
            pltpu.SemaphoreType.REGULAR,
            pltpu.SemaphoreType.REGULAR,
        ],
        compiler_params=pltpu.CompilerParams(
            collective_id=0, has_side_effects=True, vmem_limit_bytes=64_000_000
        ),
        name="exchange",
    )(dft_tables(side), pair_list, pair_count, tissue, patches)
    return pl.pallas_call(
        unpack,
        out_shape=(
            jax.ShapeDtypeStruct((1, 2, slots), F32),
            jax.ShapeDtypeStruct((1, 2, total), F32),
        ),
        in_specs=[vmem],
        out_specs=(vmem, vmem),
        compiler_params=pltpu.CompilerParams(vmem_limit_bytes=2_000_000),
        name="unpack",
    )(both)


def solution(mesh):
    return jax.shard_map(
        functools.partial(on_device, mesh.shape["sec"]),
        mesh=mesh,
        in_specs=(
            P(("group", "sec"), None, None, None),
            P(("group", "sec"), None),
            P(("group", "sec")),
            P(("group", "sec"), None),
        ),
        out_specs=(P(("group", "sec"), None, None), P(("group", "sec"), None, None)),
        check_vma=False,
    )
```

```python
import functools

import jax
import jax.numpy as jnp
import numpy as np
from jax import lax
from jax.experimental import pallas as pl
from jax.experimental.pallas import tpu as pltpu
from jax.sharding import PartitionSpec as P

GR = 8
SPRING = 0.25
STEP = 0.15
CHUNK = 8
PIECE = 2
BANDS = 2
HALO = 3
MESH = pl.DeviceIdType.MESH
F32 = jnp.float32
BF16 = jnp.bfloat16


def dft_tables(length):
    index = np.arange(length)
    angle = (index[:, None] * index[None, :] % length) * (2.0 * np.pi / length)
    c = np.cos(angle).astype(np.float32)
    s = np.sin(angle).astype(np.float32)
    right = np.concatenate([c, s], axis=1)
    left = np.block([[c, -s], [-s, -c]])
    inner = np.block([[c, s], [-s, c]])
    last = np.concatenate([c, -s], axis=1)
    tables = np.concatenate([right, left, inner, last], axis=0)
    return jnp.asarray(tables.astype(jnp.bfloat16))


def dot(a, b):
    return jnp.dot(a, b, preferred_element_type=F32)


def dot_nt(a, b):
    return lax.dot_general(a, b, (((1,), (1,)), ((), ())), preferred_element_type=F32)


def split3(x):
    top = x.astype(BF16)
    rest = x - top.astype(F32)
    mid = rest.astype(BF16)
    return top, mid, (rest - mid.astype(F32)).astype(BF16)


def stacked(both, a, b, side):
    ra = both[a * side : (a + 1) * side]
    rb = both[b * side : (b + 1) * side]
    top = jnp.concatenate([ra[:, :side], rb[:, :side]], axis=1)
    low = jnp.concatenate([ra[:, side:], rb[:, side:]], axis=1)
    return jnp.concatenate([top, low], axis=0)


def spectra(images, right, left):
    side = images[0].shape[0]
    rows = jnp.concatenate(images, axis=0)
    both = dot(rows, right).astype(BF16)
    return [dot(left, stacked(both, 2 * i, 2 * i + 1, side)) for i in range(len(images) // 2)]


def lane_roll(x, shift):
    return pltpu.roll(x, shift % x.shape[-1], x.ndim - 1)


def single(pair):
    return pair % 2


def up_chunks(pair, n, chunks):
    return chunks * ((pair + 1) // 2) // (n // 2)


def exchange(
    n,
    tables_any,
    list_any,
    count_s,
    tissue_any,
    patches_any,
    out_ref,
    patches_a,
    patches_b,
    tables,
    list_v,
    list_s,
    tissue_v,
    note,
    far_note,
    far_s,
    outgoing,
    incoming,
    own_spec,
    peak_ref,
    mass_ref,
    moment_ref,
    packet,
    halo,
    load_sems,
    list_sems,
    send_sems,
    recv_sems,
    halo_send,
    halo_recv,
    near_sem,
    far_sem,
):
    me = lax.axis_index("sec")
    patches = (patches_a, patches_b)
    total, _, side = patches_a.shape
    slots = list_v.shape[1]
    chunks = slots // CHUNK
    offsets = [d for d in range(-HALO, HALO + 1) if d != 0]

    loads = [
        pltpu.make_async_copy(source, target, load_sems.at[i])
        for i, (source, target) in enumerate(
            (
                (list_any, list_s),
                (list_any, list_v),
                (tables_any, tables),
                (tissue_any, tissue_v),
            )
        )
    ]
    loads[0].start()
    loads[1].start()
    bands = [pl.ds(i * side // BANDS, side // BANDS) for i in range(BANDS)]
    band_loads = [
        pltpu.make_async_copy(
            patches_any.at[0, :, band], patches[i], load_sems.at[4 + i]
        )
        for i, band in enumerate(bands)
    ]
    for load in band_loads:
        load.start()
    loads[2].start()
    loads[3].start()

    halo[...] = jnp.zeros_like(halo)
    far_note[...] = jnp.zeros_like(far_note)

    barrier = pltpu.get_barrier_semaphore()

    def greet(sem):
        for to in (me + 1 - 2 * (me % 2), me - 1 + 2 * (me % 2)):

            @pl.when((to >= 0) & (to < n))
            def _():
                pl.semaphore_signal(sem, inc=1, device_id={"sec": to}, device_id_type=MESH)

    greet(barrier)

    peak_ref[...] = jnp.zeros_like(peak_ref)
    mass_ref[...] = jnp.ones_like(mass_ref)
    moment_ref[...] = jnp.zeros_like(moment_ref)
    loads[0].wait()
    loads[1].wait()
    count = count_s[0]
    note[...] = jnp.concatenate([list_v[...], jnp.full((1, slots), count, jnp.int32)], axis=0)

    has_up = jnp.minimum(n - 1 - me, 1)
    has_down = jnp.minimum(me, 1)
    my_up = up_chunks(me, n, chunks)
    far_up = up_chunks(me - 1, n, chunks)
    my_half = has_up * single(me)
    far_half = has_down * single(me - 1)

    sides = jnp.minimum(me, 1) + jnp.minimum(n - 1 - me, 1)
    pl.semaphore_wait(barrier, sides)

    list_copy = pltpu.make_async_remote_copy(
        src_ref=note,
        dst_ref=far_note,
        send_sem=list_sems.at[0],
        recv_sem=list_sems.at[1],
        device_id={"sec": me + 1},
        device_id_type=MESH,
    )

    slot_copy = pltpu.make_async_remote_copy(
        src_ref=list_v,
        dst_ref=far_s,
        send_sem=list_sems.at[2],
        recv_sem=list_sems.at[3],
        device_id={"sec": me + 1},
        device_id_type=MESH,
    )

    @pl.when(me < n - 1)
    def _():
        slot_copy.start()
        list_copy.start()


    def patch_copy(q, to):
        return pltpu.make_async_remote_copy(
            src_ref=outgoing.at[pl.ds(q * CHUNK, CHUNK)],
            dst_ref=incoming.at[pl.ds(q * CHUNK, CHUNK)],
            send_sem=send_sems.at[0],
            recv_sem=recv_sems.at[q],
            device_id={"sec": to},
            device_id_type=MESH,
        )

    def piece_copy(q, first, size, to):
        at = pl.ds(q * CHUNK + first, size)
        return pltpu.make_async_remote_copy(
            src_ref=outgoing.at[at],
            dst_ref=incoming.at[at],
            send_sem=send_sems.at[0],
            recv_sem=recv_sems.at[q],
            device_id={"sec": to},
            device_id_type=MESH,
        )

    def gather(source, q, c, first, count):
        for j in range(first, first + count):
            for part, band in zip(patches, bands):
                outgoing[q * CHUNK + j, band] = part[source[0, c * CHUNK + j]]

    def send_up(c, carry):
        gather(list_s, c, c, 0, CHUNK)
        patch_copy(c, me + 1).start()
        return carry

    for i, band in enumerate(bands):
        band_loads[i].wait()

        @pl.when(has_up * my_up > 0)
        def _():
            for j in range(CHUNK):
                outgoing[j, band] = patches[i][list_s[0, j]]
            pltpu.make_async_remote_copy(
                src_ref=outgoing.at[0:CHUNK, band],
                dst_ref=incoming.at[0:CHUNK, band],
                send_sem=send_sems.at[0],
                recv_sem=recv_sems.at[0],
                device_id={"sec": me + 1},
                device_id_type=MESH,
            ).start()

    lax.fori_loop(1, has_up * my_up, send_up, 0)

    @pl.when(my_half > 0)
    def _():
        gather(list_s, my_up, my_up, 0, PIECE)
        piece_copy(my_up, 0, PIECE, me + 1).start()

    greet(near_sem)
    right_ref = tables.at[0:side]
    left_ref = tables.at[side : 3 * side]
    inner_ref = tables.at[3 * side : 5 * side]
    last_ref = tables.at[5 * side : 6 * side]

    def own_group(q, carry):
        images = []
        for j in range(CHUNK):
            far = far_s[0, jnp.minimum(q, chunks - 1) * CHUNK + j]
            near = list_s[0, jnp.maximum(q - chunks, 0) * CHUNK + j]
            at = jnp.where(q < chunks, far, near)
            images.append(jnp.concatenate([part[at] for part in patches], axis=0))
        for i, spec in enumerate(spectra(images, right_ref[...], left_ref[...])):
            own_spec[q * (CHUNK // 2) + i] = spec.astype(BF16)
        return carry

    @pl.when(me > 0)
    def _():
        slot_copy.wait_recv()

    @pl.when(me == 0)
    def _():
        fill = pltpu.make_async_copy(list_v, far_s, list_sems.at[3])
        fill.start()
        fill.wait()

    @pl.when(far_half > 0)
    def _():
        gather(far_s, chunks + far_up, far_up, PIECE, CHUNK - PIECE)
        piece_copy(chunks + far_up, PIECE, CHUNK - PIECE, me - 1).start()

    down_from = far_up + far_half

    def send_down(c, carry):
        gather(far_s, chunks + c, c, 0, CHUNK)
        patch_copy(chunks + c, me - 1).start()
        return carry

    lax.fori_loop(down_from, down_from + has_down * (chunks - down_from), send_down, 0)
    for load in loads[2:]:
        load.wait()
    lax.fori_loop(chunks + my_up, chunks + my_up + has_up * (chunks - my_up), own_group, 0)
    lax.fori_loop(0, has_down * far_up + far_half, own_group, 0)

    pl.semaphore_wait(near_sem, sides)
    greet(far_sem)
    @pl.when(me > 0)
    def _():
        list_copy.wait_recv()

    half = side // 2
    row = lax.broadcasted_iota(jnp.int32, (side, 1), 0)
    row_lag = ((row + half) % side - half).astype(F32)
    scale = 64.0 / float(side * side * side * side)

    def match_group(t, carry):
        start_a, count_a, start_b = carry
        q = jnp.where(t < count_a, start_a + t, start_b + t - count_a)
        is_far_half = (q == far_up) & (far_half > 0)
        is_my_half = (q == chunks + my_up) & (my_half > 0)

        @pl.when(is_far_half)
        def _():
            piece_copy(q, 0, PIECE, me).wait_recv()

        @pl.when(is_my_half)
        def _():
            piece_copy(q, PIECE, CHUNK - PIECE, me).wait_recv()

        @pl.when(jnp.logical_not(is_far_half | is_my_half))
        def _():
            patch_copy(q, me).wait_recv()

        sign = jnp.where(q < chunks, -1.0, 1.0).astype(F32)
        images = [incoming[q * CHUNK + j] for j in range(CHUNK)]
        crosses = []
        for i, spec in enumerate(spectra(images, right_ref[...], left_ref[...])):
            ar = spec[:side].astype(BF16).astype(F32)
            ai = spec[side:].astype(BF16).astype(F32)
            own = own_spec[q * (CHUNK // 2) + i].astype(F32)
            br, bi = own[:side], own[side:]
            cr = (br * ar + bi * ai).astype(BF16)
            ci = ((br * ai - bi * ar) * sign).astype(BF16)
            crosses.append(jnp.concatenate([cr[:, :side], ci[:, :side]], axis=1))
            crosses.append(jnp.concatenate([cr[:, side:], ci[:, side:]], axis=1))
        inner = dot(jnp.concatenate(crosses, axis=0), inner_ref[...]).astype(BF16)
        peaks, masses, moments = [], [], []
        for i in range(CHUNK // 2):
            scores = dot(last_ref[...], stacked(inner, 2 * i, 2 * i + 1, side)) * scale
            peak = jnp.max(scores, axis=0, keepdims=True)
            e = jnp.exp(scores - peak)
            mass = jnp.sum(e, axis=0, keepdims=True)
            moment = jnp.sum(e * row_lag, axis=0, keepdims=True)
            for parts, value in ((peaks, peak), (masses, mass), (moments, moment)):
                parts.append(value[:, :side])
                parts.append(value[:, side:])
        at = pl.ds(pl.multiple_of(q * CHUNK, CHUNK), CHUNK)
        peak_ref[at, :] = jnp.concatenate(peaks, axis=0)
        mass_ref[at, :] = jnp.concatenate(masses, axis=0)
        moment_ref[at, :] = jnp.concatenate(moments, axis=0)
        return carry

    n_far = has_down * far_up + far_half
    n_near = has_up * (chunks - my_up)
    odd = me % 2
    start_a = (1 - odd) * (chunks + my_up)
    start_b = odd * (chunks + my_up)
    count_a = odd * n_far + (1 - odd) * n_near
    lax.fori_loop(0, n_far + n_near, match_group, (start_a, count_a, start_b))

    peak = peak_ref[...]
    weight = jnp.exp(peak - jnp.max(peak, axis=1, keepdims=True))
    mass = mass_ref[...] * weight
    moment = moment_ref[...] * weight
    col = lax.broadcasted_iota(jnp.int32, (8, side), 1)
    sub = lax.broadcasted_iota(jnp.int32, (8, side), 0)
    col_lag = ((col + half) % side - half).astype(F32)
    axes = jnp.where(sub == 0, 1.0, jnp.where(sub == 1, col_lag, 0.0))
    thirds = jnp.concatenate(split3(jnp.concatenate([mass, moment], axis=0)), axis=0)
    triple = dot_nt(axes.astype(BF16), thirds)
    span = 4 * slots
    joined = triple[:, 0:span] + triple[:, span : 2 * span] + triple[:, 2 * span :]
    sums, rows_num = joined[:, 0 : 2 * slots], joined[:, 2 * slots :]
    mass_all = sums[0:1]
    place = lax.broadcasted_iota(jnp.int32, (1, 2 * slots), 1)
    is_far = place < slots
    far = far_note[...]
    counts = jnp.concatenate([far[1:2], jnp.full((1, slots), count, jnp.int32)], axis=1)
    lists = jnp.concatenate([far[0:1], list_v[...]], axis=1)
    slot = jnp.where(is_far, place, place - slots)
    first = jnp.where(is_far, 0, (chunks - n_near) * CHUNK + my_half * PIECE)
    stop = jnp.minimum(jnp.where(is_far, n_far * CHUNK - far_half * (CHUNK - PIECE), slots), counts)
    live = (slot >= first) & (slot < stop)
    flow_rows = jnp.where(live, rows_num[0:1] / mass_all, 0.0)
    flow_cols = jnp.where(live, sums[1:2] / mass_all, 0.0)
    which = lax.broadcasted_iota(jnp.int32, (total, 2 * slots), 0)
    onehot = (which == lists).astype(F32).astype(BF16)
    one_pair = jnp.concatenate(
        [flow_rows, flow_cols, live.astype(F32), jnp.zeros((5, 2 * slots), F32)], axis=0
    )
    both = jnp.concatenate(
        [jnp.where(is_far, one_pair, 0.0), jnp.where(is_far, 0.0, one_pair)], axis=0
    )
    triple = dot_nt(jnp.concatenate(split3(both), axis=0), onehot)
    field = triple[0:16] + triple[16:32] + triple[32:48]
    packet[0:3] = field[0:3]
    packet[3:4] = tissue_v[...].astype(F32)
    packet[4:8] = field[4:8]
    packet[8:16] = field[8:16]
    packet[4:5, 0 : 2 * slots] = flow_rows
    packet[5:6, 0 : 2 * slots] = flow_cols

    pl.semaphore_wait(far_sem, sides)

    def halo_copy(d):
        return pltpu.make_async_remote_copy(
            src_ref=packet,
            dst_ref=halo.at[HALO - d],
            send_sem=halo_send.at[0],
            recv_sem=halo_recv.at[HALO - d],
            device_id={"sec": me + d},
            device_id_type=MESH,
        )

    for d in offsets:

        @pl.when((me + d >= 0) & (me + d < n))
        def _():
            halo_copy(d).start()

    @pl.when(me < n - 1)
    def _():
        slot_copy.wait_send()
        list_copy.wait_send()

    def drain_up(c, carry):
        patch_copy(c, me + 1).wait_send()
        return carry

    lax.fori_loop(0, has_up * my_up, drain_up, 0)

    @pl.when(my_half > 0)
    def _():
        piece_copy(my_up, 0, PIECE, me + 1).wait_send()

    def drain_down(c, carry):
        patch_copy(chunks + c, me - 1).wait_send()
        return carry

    lax.fori_loop(down_from, down_from + has_down * (chunks - down_from), drain_down, 0)

    @pl.when(far_half > 0)
    def _():
        piece_copy(chunks + far_up, PIECE, CHUNK - PIECE, me - 1).wait_send()

    for d in offsets:

        @pl.when((me - d >= 0) & (me - d < n))
        def _():
            halo_copy(d).wait_recv()

    halo[HALO] = packet[...]
    relax(slots, halo, out_ref)
    for d in offsets:

        @pl.when((me + d >= 0) & (me + d < n))
        def _():
            halo_copy(d).wait_send()


def relax(slots, halo, out_ref):
    total = halo.shape[-1]
    near, above = halo[HALO], halo[HALO + 1]
    out_ref[2:4, 0:slots] = near[4:6, slots : 2 * slots] + above[4:6, 0:slots]
    fields = {d: halo[HALO + d][8:16] + halo[HALO + d + 1][0:8] for d in range(-HALO, HALO)}
    links = {d: jnp.broadcast_to(f[2:3], f.shape) for d, f in fields.items()}
    lane = lax.broadcasted_iota(jnp.int32, (8, total), 1)
    width = total // GR
    has_right = (lane % width) != width - 1
    has_below = lane < total - width

    def springs(d):
        tissue = jnp.broadcast_to(halo[HALO + d][3:4], (8, total))
        stiff = SPRING * (1.0 + 2.0 * tissue)
        across = jnp.where(has_right, 0.5 * (stiff + lane_roll(stiff, -1)), 0.0)
        along = jnp.where(has_below, 0.5 * (stiff + lane_roll(stiff, -width)), 0.0)
        return across, along

    def plane(u, spring):
        across, along = spring
        a = across * (lane_roll(u, -1) - u)
        b = along * (lane_roll(u, -width) - u)
        return (lane_roll(a, 1) - a) + (lane_roll(b, width) - b)

    spring = {d: springs(d) for d in (-1, 0, 1)}
    pull = {d: links[d] * fields[d] for d in fields}
    u1 = {d: -STEP * (pull[d] - pull[d - 1]) for d in range(-2, 3)}

    def relaxed(u, d):
        gap_here = u[d + 1] - u[d] - fields[d]
        gap_below = u[d] - u[d - 1] - fields[d - 1]
        force = plane(u[d], spring[d]) - links[d] * gap_here + links[d - 1] * gap_below
        return u[d] - STEP * force

    u2 = {d: relaxed(u1, d) for d in (-1, 0, 1)}
    out_ref[0:2] = relaxed(u2, 0)[0:2]


def unpack(both, flow_ref, pos_ref):
    flow_ref[0] = both[2:4, 0 : flow_ref.shape[-1]]
    pos_ref[0] = both[0:2]


def on_device(n, patches, pair_list, pair_count, tissue):
    _, total, side, _ = patches.shape
    slots = pair_list.shape[1]
    chunks = slots // CHUNK
    vmem = pl.BlockSpec(memory_space=pltpu.VMEM)
    any_space = pl.BlockSpec(memory_space=pl.ANY)
    dma = pltpu.SemaphoreType.DMA
    both = pl.pallas_call(
        functools.partial(exchange, n),
        out_shape=pltpu.VMEM((4, total), F32),
        in_specs=[any_space] * 2 + [pl.BlockSpec(memory_space=pltpu.SMEM)] + [any_space] * 2,
        out_specs=vmem,
        scratch_shapes=[
            pltpu.VMEM((total, side // BANDS, side), BF16),
            pltpu.VMEM((total, side // BANDS, side), BF16),
            pltpu.VMEM((6 * side, 2 * side), BF16),
            pltpu.VMEM((1, slots), jnp.int32),
            pltpu.SMEM((1, slots), jnp.int32),
            pltpu.VMEM((1, total), jnp.int32),
            pltpu.VMEM((2, slots), jnp.int32),
            pltpu.VMEM((2, slots), jnp.int32),
            pltpu.SMEM((1, slots), jnp.int32),
            pltpu.VMEM((2 * slots, side, side), BF16),
            pltpu.VMEM((2 * slots, side, side), BF16),
            pltpu.VMEM((slots, 2 * side, 2 * side), BF16),
            pltpu.VMEM((2 * slots, side), F32),
            pltpu.VMEM((2 * slots, side), F32),
            pltpu.VMEM((2 * slots, side), F32),
            pltpu.VMEM((16, total), F32),
            pltpu.VMEM((2 * HALO + 1, 16, total), F32),
            dma((4 + BANDS,)),
            dma((4,)),
            dma((1,)),
            dma((2 * chunks,)),
            dma((1,)),
            dma((2 * HALO + 1,)),
            pltpu.SemaphoreType.REGULAR,
            pltpu.SemaphoreType.REGULAR,
        ],
        compiler_params=pltpu.CompilerParams(
            collective_id=0, has_side_effects=True, vmem_limit_bytes=64_000_000
        ),
        name="exchange",
    )(dft_tables(side), pair_list, pair_count, tissue, patches)
    return pl.pallas_call(
        unpack,
        out_shape=(
            jax.ShapeDtypeStruct((1, 2, slots), F32),
            jax.ShapeDtypeStruct((1, 2, total), F32),
        ),
        in_specs=[vmem],
        out_specs=(vmem, vmem),
        compiler_params=pltpu.CompilerParams(vmem_limit_bytes=2_000_000),
        name="unpack",
    )(both)


def solution(mesh):
    return jax.shard_map(
        functools.partial(on_device, mesh.shape["sec"]),
        mesh=mesh,
        in_specs=(
            P(("group", "sec"), None, None, None),
            P(("group", "sec"), None),
            P(("group", "sec")),
            P(("group", "sec"), None),
        ),
        out_specs=(P(("group", "sec"), None, None), P(("group", "sec"), None, None)),
        check_vma=False,
    )
```

```python
import functools

import jax
import jax.numpy as jnp
import numpy as np
from jax import lax
from jax.experimental import pallas as pl
from jax.experimental.pallas import tpu as pltpu
from jax.sharding import PartitionSpec as P

GR = 8
SPRING = 0.25
STEP = 0.15
CHUNK = 8
PIECE = 2
HALF = CHUNK // 2
BANDS = 2
HALO = 3
MESH = pl.DeviceIdType.MESH
F32 = jnp.float32
BF16 = jnp.bfloat16


def dft_tables(length):
    index = np.arange(length)
    angle = (index[:, None] * index[None, :] % length) * (2.0 * np.pi / length)
    c = np.cos(angle).astype(np.float32)
    s = np.sin(angle).astype(np.float32)
    right = np.concatenate([c, s], axis=1)
    left = np.block([[c, -s], [-s, -c]])
    inner = np.block([[c, s], [-s, c]])
    last = np.concatenate([c, -s], axis=1)
    tables = np.concatenate([right, left, inner, last], axis=0)
    return jnp.asarray(tables.astype(jnp.bfloat16))


def dot(a, b):
    return jnp.dot(a, b, preferred_element_type=F32)


def dot_nt(a, b):
    return lax.dot_general(a, b, (((1,), (1,)), ((), ())), preferred_element_type=F32)


def split3(x):
    top = x.astype(BF16)
    rest = x - top.astype(F32)
    mid = rest.astype(BF16)
    return top, mid, (rest - mid.astype(F32)).astype(BF16)


def stacked(both, a, b, side):
    ra = both[a * side : (a + 1) * side]
    rb = both[b * side : (b + 1) * side]
    top = jnp.concatenate([ra[:, :side], rb[:, :side]], axis=1)
    low = jnp.concatenate([ra[:, side:], rb[:, side:]], axis=1)
    return jnp.concatenate([top, low], axis=0)


def spectra(images, right, left):
    side = images[0].shape[0]
    rows = jnp.concatenate(images, axis=0)
    both = dot(rows, right).astype(BF16)
    return [dot(left, stacked(both, 2 * i, 2 * i + 1, side)) for i in range(len(images) // 2)]


def lane_roll(x, shift):
    return pltpu.roll(x, shift % x.shape[-1], x.ndim - 1)


def single(pair):
    return pair % 2


def up_chunks(pair, n, chunks):
    return chunks * ((pair + 1) // 2) // (n // 2)


def exchange(
    n,
    tables_any,
    list_any,
    count_s,
    tissue_any,
    patches_any,
    out_ref,
    patches_a,
    patches_b,
    tables,
    list_v,
    list_s,
    tissue_v,
    note,
    far_note,
    far_s,
    outgoing,
    incoming,
    own_spec,
    peak_ref,
    mass_ref,
    moment_ref,
    packet,
    halo,
    load_sems,
    list_sems,
    send_sems,
    recv_sems,
    halo_send,
    halo_recv,
    near_sem,
    far_sem,
):
    me = lax.axis_index("sec")
    patches = (patches_a, patches_b)
    total, _, side = patches_a.shape
    slots = list_v.shape[1]
    chunks = slots // CHUNK
    offsets = [d for d in range(-HALO, HALO + 1) if d != 0]

    loads = [
        pltpu.make_async_copy(source, target, load_sems.at[i])
        for i, (source, target) in enumerate(
            (
                (list_any, list_s),
                (list_any, list_v),
                (tables_any, tables),
                (tissue_any, tissue_v),
            )
        )
    ]
    loads[0].start()
    loads[1].start()
    bands = [pl.ds(i * side // BANDS, side // BANDS) for i in range(BANDS)]
    band_loads = [
        pltpu.make_async_copy(
            patches_any.at[0, :, band], patches[i], load_sems.at[4 + i]
        )
        for i, band in enumerate(bands)
    ]
    for load in band_loads:
        load.start()
    loads[2].start()
    loads[3].start()

    halo[...] = jnp.zeros_like(halo)
    far_note[...] = jnp.zeros_like(far_note)

    barrier = pltpu.get_barrier_semaphore()

    def greet(sem):
        for to in (me + 1 - 2 * (me % 2), me - 1 + 2 * (me % 2)):

            @pl.when((to >= 0) & (to < n))
            def _():
                pl.semaphore_signal(sem, inc=1, device_id={"sec": to}, device_id_type=MESH)

    greet(barrier)

    peak_ref[...] = jnp.zeros_like(peak_ref)
    mass_ref[...] = jnp.ones_like(mass_ref)
    moment_ref[...] = jnp.zeros_like(moment_ref)
    loads[0].wait()
    loads[1].wait()
    count = count_s[0]
    note[...] = jnp.concatenate([list_v[...], jnp.full((1, slots), count, jnp.int32)], axis=0)

    has_up = jnp.minimum(n - 1 - me, 1)
    has_down = jnp.minimum(me, 1)
    my_up = up_chunks(me, n, chunks)
    far_up = up_chunks(me - 1, n, chunks)
    tail_near = has_up * (me % 2) * jnp.minimum(chunks - 1 - my_up, 1)
    tail_far = has_down * (1 - me % 2) * jnp.minimum(chunks - 1 - far_up, 1)
    my_half = has_up * single(me)
    far_half = has_down * single(me - 1)

    sides = jnp.minimum(me, 1) + jnp.minimum(n - 1 - me, 1)
    pl.semaphore_wait(barrier, sides)

    list_copy = pltpu.make_async_remote_copy(
        src_ref=note,
        dst_ref=far_note,
        send_sem=list_sems.at[0],
        recv_sem=list_sems.at[1],
        device_id={"sec": me + 1},
        device_id_type=MESH,
    )

    slot_copy = pltpu.make_async_remote_copy(
        src_ref=list_v,
        dst_ref=far_s,
        send_sem=list_sems.at[2],
        recv_sem=list_sems.at[3],
        device_id={"sec": me + 1},
        device_id_type=MESH,
    )

    @pl.when(me < n - 1)
    def _():
        slot_copy.start()
        list_copy.start()


    def patch_copy(q, to):
        return pltpu.make_async_remote_copy(
            src_ref=outgoing.at[pl.ds(q * CHUNK, CHUNK)],
            dst_ref=incoming.at[pl.ds(q * CHUNK, CHUNK)],
            send_sem=send_sems.at[0],
            recv_sem=recv_sems.at[q],
            device_id={"sec": to},
            device_id_type=MESH,
        )

    def half_copy(i, to):
        at = pl.ds(2 * slots - CHUNK + i * HALF, HALF)
        return pltpu.make_async_remote_copy(
            src_ref=outgoing.at[at],
            dst_ref=incoming.at[at],
            send_sem=send_sems.at[0],
            recv_sem=recv_sems.at[2 * chunks - 1 + i],
            device_id={"sec": to},
            device_id_type=MESH,
        )

    def piece_copy(q, first, size, to):
        at = pl.ds(q * CHUNK + first, size)
        return pltpu.make_async_remote_copy(
            src_ref=outgoing.at[at],
            dst_ref=incoming.at[at],
            send_sem=send_sems.at[0],
            recv_sem=recv_sems.at[q],
            device_id={"sec": to},
            device_id_type=MESH,
        )

    def gather(source, q, c, first, count):
        for j in range(first, first + count):
            for part, band in zip(patches, bands):
                outgoing[q * CHUNK + j, band] = part[source[0, c * CHUNK + j]]

    def send_up(c, carry):
        gather(list_s, c, c, 0, CHUNK)
        patch_copy(c, me + 1).start()
        return carry

    for i, band in enumerate(bands):
        band_loads[i].wait()

        @pl.when(has_up * my_up > 0)
        def _():
            for j in range(CHUNK):
                outgoing[j, band] = patches[i][list_s[0, j]]
            pltpu.make_async_remote_copy(
                src_ref=outgoing.at[0:CHUNK, band],
                dst_ref=incoming.at[0:CHUNK, band],
                send_sem=send_sems.at[0],
                recv_sem=recv_sems.at[0],
                device_id={"sec": me + 1},
                device_id_type=MESH,
            ).start()

    lax.fori_loop(1, has_up * my_up, send_up, 0)

    @pl.when(my_half > 0)
    def _():
        gather(list_s, my_up, my_up, 0, PIECE)
        piece_copy(my_up, 0, PIECE, me + 1).start()

    greet(near_sem)
    right_ref = tables.at[0:side]
    left_ref = tables.at[side : 3 * side]
    inner_ref = tables.at[3 * side : 5 * side]
    last_ref = tables.at[5 * side : 6 * side]

    def own_group(q, carry):
        images = []
        for j in range(CHUNK):
            far = far_s[0, jnp.minimum(q, chunks - 1) * CHUNK + j]
            near = list_s[0, jnp.maximum(q - chunks, 0) * CHUNK + j]
            at = jnp.where(q < chunks, far, near)
            images.append(jnp.concatenate([part[at] for part in patches], axis=0))
        for i, spec in enumerate(spectra(images, right_ref[...], left_ref[...])):
            own_spec[q * (CHUNK // 2) + i] = spec.astype(BF16)
        return carry

    @pl.when(me > 0)
    def _():
        slot_copy.wait_recv()

    @pl.when(me == 0)
    def _():
        fill = pltpu.make_async_copy(list_v, far_s, list_sems.at[3])
        fill.start()
        fill.wait()

    @pl.when(far_half > 0)
    def _():
        gather(far_s, chunks + far_up, far_up, PIECE, CHUNK - PIECE)
        piece_copy(chunks + far_up, PIECE, CHUNK - PIECE, me - 1).start()

    down_from = far_up + far_half

    def send_down(c, carry):
        gather(far_s, chunks + c, c, 0, CHUNK)
        patch_copy(chunks + c, me - 1).start()
        return carry

    n_down = has_down * (chunks - down_from) - tail_far
    lax.fori_loop(down_from, down_from + n_down, send_down, 0)

    @pl.when(tail_far > 0)
    def _():
        for i in range(2):
            gather(far_s, 2 * chunks - 1, chunks - 1, i * HALF, HALF)
            half_copy(i, me - 1).start()

    for load in loads[2:]:
        load.wait()
    lax.fori_loop(chunks + my_up, chunks + my_up + has_up * (chunks - my_up), own_group, 0)
    lax.fori_loop(0, has_down * far_up + far_half, own_group, 0)

    pl.semaphore_wait(near_sem, sides)
    greet(far_sem)
    @pl.when(me > 0)
    def _():
        list_copy.wait_recv()

    half = side // 2
    row = lax.broadcasted_iota(jnp.int32, (side, 1), 0)
    row_lag = ((row + half) % side - half).astype(F32)
    scale = 64.0 / float(side * side * side * side)

    def match(slot, size):
        sign = jnp.where(slot < slots, -1.0, 1.0).astype(F32)
        images = [incoming[slot + j] for j in range(size)]
        crosses = []
        for i, spec in enumerate(spectra(images, right_ref[...], left_ref[...])):
            ar = spec[:side].astype(BF16).astype(F32)
            ai = spec[side:].astype(BF16).astype(F32)
            own = own_spec[slot // 2 + i].astype(F32)
            br, bi = own[:side], own[side:]
            cr = (br * ar + bi * ai).astype(BF16)
            ci = ((br * ai - bi * ar) * sign).astype(BF16)
            crosses.append(jnp.concatenate([cr[:, :side], ci[:, :side]], axis=1))
            crosses.append(jnp.concatenate([cr[:, side:], ci[:, side:]], axis=1))
        inner = dot(jnp.concatenate(crosses, axis=0), inner_ref[...]).astype(BF16)
        peaks, masses, moments = [], [], []
        for i in range(size // 2):
            scores = dot(last_ref[...], stacked(inner, 2 * i, 2 * i + 1, side)) * scale
            peak = jnp.max(scores, axis=0, keepdims=True)
            e = jnp.exp(scores - peak)
            mass = jnp.sum(e, axis=0, keepdims=True)
            moment = jnp.sum(e * row_lag, axis=0, keepdims=True)
            for parts, value in ((peaks, peak), (masses, mass), (moments, moment)):
                parts.append(value[:, :side])
                parts.append(value[:, side:])
        at = pl.ds(slot, size)
        peak_ref[at, :] = jnp.concatenate(peaks, axis=0)
        mass_ref[at, :] = jnp.concatenate(masses, axis=0)
        moment_ref[at, :] = jnp.concatenate(moments, axis=0)

    def match_group(t, carry):
        start_a, count_a, start_b = carry
        q = jnp.where(t < count_a, start_a + t, start_b + t - count_a)
        is_my_half = (q == chunks + my_up) & (my_half > 0)

        @pl.when(is_my_half)
        def _():
            piece_copy(q, PIECE, CHUNK - PIECE, me).wait_recv()

        @pl.when(jnp.logical_not(is_my_half))
        def _():
            patch_copy(q, me).wait_recv()

        match(pl.multiple_of(q * CHUNK, CHUNK), CHUNK)
        return carry

    n_far = has_down * far_up + far_half
    n_near = has_up * (chunks - my_up)
    odd = me % 2
    start_a = (1 - odd) * (chunks + my_up)
    start_b = odd * (chunks + my_up)
    count_a = odd * n_far + (1 - odd) * n_near
    n_main = n_far + n_near - far_half - tail_near
    lax.fori_loop(0, n_main, match_group, (start_a, count_a, start_b))

    def match_tail(i, carry):
        @pl.when(far_half > 0)
        def _():
            piece_copy(far_up, 0, PIECE, me).wait_recv()

        for k in range(2):

            @pl.when((tail_near > 0) & (i == k))
            def _():
                half_copy(k, me).wait_recv()

        near_slot = 2 * slots - CHUNK + i * HALF
        match(pl.multiple_of(jnp.where(far_half > 0, far_up * CHUNK, near_slot), HALF), HALF)
        return carry

    lax.fori_loop(0, far_half + 2 * tail_near, match_tail, 0)

    peak = peak_ref[...]
    weight = jnp.exp(peak - jnp.max(peak, axis=1, keepdims=True))
    mass = mass_ref[...] * weight
    moment = moment_ref[...] * weight
    col = lax.broadcasted_iota(jnp.int32, (8, side), 1)
    sub = lax.broadcasted_iota(jnp.int32, (8, side), 0)
    col_lag = ((col + half) % side - half).astype(F32)
    axes = jnp.where(sub == 0, 1.0, jnp.where(sub == 1, col_lag, 0.0))
    thirds = jnp.concatenate(split3(jnp.concatenate([mass, moment], axis=0)), axis=0)
    triple = dot_nt(axes.astype(BF16), thirds)
    span = 4 * slots
    joined = triple[:, 0:span] + triple[:, span : 2 * span] + triple[:, 2 * span :]
    sums, rows_num = joined[:, 0 : 2 * slots], joined[:, 2 * slots :]
    mass_all = sums[0:1]
    place = lax.broadcasted_iota(jnp.int32, (1, 2 * slots), 1)
    is_far = place < slots
    far = far_note[...]
    counts = jnp.concatenate([far[1:2], jnp.full((1, slots), count, jnp.int32)], axis=1)
    lists = jnp.concatenate([far[0:1], list_v[...]], axis=1)
    slot = jnp.where(is_far, place, place - slots)
    first = jnp.where(is_far, 0, (chunks - n_near) * CHUNK + my_half * PIECE)
    stop = jnp.minimum(jnp.where(is_far, n_far * CHUNK - far_half * (CHUNK - PIECE), slots), counts)
    live = (slot >= first) & (slot < stop)
    flow_rows = jnp.where(live, rows_num[0:1] / mass_all, 0.0)
    flow_cols = jnp.where(live, sums[1:2] / mass_all, 0.0)
    which = lax.broadcasted_iota(jnp.int32, (total, 2 * slots), 0)
    onehot = (which == lists).astype(F32).astype(BF16)
    one_pair = jnp.concatenate(
        [flow_rows, flow_cols, live.astype(F32), jnp.zeros((5, 2 * slots), F32)], axis=0
    )
    both = jnp.concatenate(
        [jnp.where(is_far, one_pair, 0.0), jnp.where(is_far, 0.0, one_pair)], axis=0
    )
    triple = dot_nt(jnp.concatenate(split3(both), axis=0), onehot)
    field = triple[0:16] + triple[16:32] + triple[32:48]
    packet[0:3] = field[0:3]
    packet[3:4] = tissue_v[...].astype(F32)
    packet[4:8] = field[4:8]
    packet[8:16] = field[8:16]
    packet[4:5, 0 : 2 * slots] = flow_rows
    packet[5:6, 0 : 2 * slots] = flow_cols

    pl.semaphore_wait(far_sem, sides)

    def halo_copy(d):
        return pltpu.make_async_remote_copy(
            src_ref=packet,
            dst_ref=halo.at[HALO - d],
            send_sem=halo_send.at[0],
            recv_sem=halo_recv.at[HALO - d],
            device_id={"sec": me + d},
            device_id_type=MESH,
        )

    for d in offsets:

        @pl.when((me + d >= 0) & (me + d < n))
        def _():
            halo_copy(d).start()

    @pl.when(me < n - 1)
    def _():
        slot_copy.wait_send()
        list_copy.wait_send()

    def drain_up(c, carry):
        patch_copy(c, me + 1).wait_send()
        return carry

    lax.fori_loop(0, has_up * my_up, drain_up, 0)

    @pl.when(my_half > 0)
    def _():
        piece_copy(my_up, 0, PIECE, me + 1).wait_send()

    def drain_down(c, carry):
        patch_copy(chunks + c, me - 1).wait_send()
        return carry

    lax.fori_loop(down_from, down_from + n_down, drain_down, 0)

    @pl.when(tail_far > 0)
    def _():
        for i in range(2):
            half_copy(i, me - 1).wait_send()

    @pl.when(far_half > 0)
    def _():
        piece_copy(chunks + far_up, PIECE, CHUNK - PIECE, me - 1).wait_send()

    for d in offsets:

        @pl.when((me - d >= 0) & (me - d < n))
        def _():
            halo_copy(d).wait_recv()

    halo[HALO] = packet[...]
    relax(slots, halo, out_ref)
    for d in offsets:

        @pl.when((me + d >= 0) & (me + d < n))
        def _():
            halo_copy(d).wait_send()


def relax(slots, halo, out_ref):
    total = halo.shape[-1]
    near, above = halo[HALO], halo[HALO + 1]
    out_ref[2:4, 0:slots] = near[4:6, slots : 2 * slots] + above[4:6, 0:slots]
    fields = {d: halo[HALO + d][8:16] + halo[HALO + d + 1][0:8] for d in range(-HALO, HALO)}
    links = {d: jnp.broadcast_to(f[2:3], f.shape) for d, f in fields.items()}
    lane = lax.broadcasted_iota(jnp.int32, (8, total), 1)
    width = total // GR
    has_right = (lane % width) != width - 1
    has_below = lane < total - width

    def springs(d):
        tissue = jnp.broadcast_to(halo[HALO + d][3:4], (8, total))
        stiff = SPRING * (1.0 + 2.0 * tissue)
        across = jnp.where(has_right, 0.5 * (stiff + lane_roll(stiff, -1)), 0.0)
        along = jnp.where(has_below, 0.5 * (stiff + lane_roll(stiff, -width)), 0.0)
        return across, along

    def plane(u, spring):
        across, along = spring
        a = across * (lane_roll(u, -1) - u)
        b = along * (lane_roll(u, -width) - u)
        return (lane_roll(a, 1) - a) + (lane_roll(b, width) - b)

    spring = {d: springs(d) for d in (-1, 0, 1)}
    pull = {d: links[d] * fields[d] for d in fields}
    u1 = {d: -STEP * (pull[d] - pull[d - 1]) for d in range(-2, 3)}

    def relaxed(u, d):
        gap_here = u[d + 1] - u[d] - fields[d]
        gap_below = u[d] - u[d - 1] - fields[d - 1]
        force = plane(u[d], spring[d]) - links[d] * gap_here + links[d - 1] * gap_below
        return u[d] - STEP * force

    u2 = {d: relaxed(u1, d) for d in (-1, 0, 1)}
    out_ref[0:2] = relaxed(u2, 0)[0:2]


def unpack(both, flow_ref, pos_ref):
    flow_ref[0] = both[2:4, 0 : flow_ref.shape[-1]]
    pos_ref[0] = both[0:2]


def on_device(n, patches, pair_list, pair_count, tissue):
    _, total, side, _ = patches.shape
    slots = pair_list.shape[1]
    chunks = slots // CHUNK
    vmem = pl.BlockSpec(memory_space=pltpu.VMEM)
    any_space = pl.BlockSpec(memory_space=pl.ANY)
    dma = pltpu.SemaphoreType.DMA
    both = pl.pallas_call(
        functools.partial(exchange, n),
        out_shape=pltpu.VMEM((4, total), F32),
        in_specs=[any_space] * 2 + [pl.BlockSpec(memory_space=pltpu.SMEM)] + [any_space] * 2,
        out_specs=vmem,
        scratch_shapes=[
            pltpu.VMEM((total, side // BANDS, side), BF16),
            pltpu.VMEM((total, side // BANDS, side), BF16),
            pltpu.VMEM((6 * side, 2 * side), BF16),
            pltpu.VMEM((1, slots), jnp.int32),
            pltpu.SMEM((1, slots), jnp.int32),
            pltpu.VMEM((1, total), jnp.int32),
            pltpu.VMEM((2, slots), jnp.int32),
            pltpu.VMEM((2, slots), jnp.int32),
            pltpu.SMEM((1, slots), jnp.int32),
            pltpu.VMEM((2 * slots, side, side), BF16),
            pltpu.VMEM((2 * slots, side, side), BF16),
            pltpu.VMEM((slots, 2 * side, 2 * side), BF16),
            pltpu.VMEM((2 * slots, side), F32),
            pltpu.VMEM((2 * slots, side), F32),
            pltpu.VMEM((2 * slots, side), F32),
            pltpu.VMEM((16, total), F32),
            pltpu.VMEM((2 * HALO + 1, 16, total), F32),
            dma((4 + BANDS,)),
            dma((4,)),
            dma((1,)),
            dma((2 * chunks + 1,)),
            dma((1,)),
            dma((2 * HALO + 1,)),
            pltpu.SemaphoreType.REGULAR,
            pltpu.SemaphoreType.REGULAR,
        ],
        compiler_params=pltpu.CompilerParams(
            collective_id=0, has_side_effects=True, vmem_limit_bytes=64_000_000
        ),
        name="exchange",
    )(dft_tables(side), pair_list, pair_count, tissue, patches)
    return pl.pallas_call(
        unpack,
        out_shape=(
            jax.ShapeDtypeStruct((1, 2, slots), F32),
            jax.ShapeDtypeStruct((1, 2, total), F32),
        ),
        in_specs=[vmem],
        out_specs=(vmem, vmem),
        compiler_params=pltpu.CompilerParams(vmem_limit_bytes=2_000_000),
        name="unpack",
    )(both)


def solution(mesh):
    return jax.shard_map(
        functools.partial(on_device, mesh.shape["sec"]),
        mesh=mesh,
        in_specs=(
            P(("group", "sec"), None, None, None),
            P(("group", "sec"), None),
            P(("group", "sec")),
            P(("group", "sec"), None),
        ),
        out_specs=(P(("group", "sec"), None, None), P(("group", "sec"), None, None)),
        check_vma=False,
    )
```

```python
import functools

import jax
import jax.numpy as jnp
import numpy as np
from jax import lax
from jax.experimental import pallas as pl
from jax.experimental.pallas import tpu as pltpu
from jax.sharding import PartitionSpec as P

GR = 8
SPRING = 0.25
STEP = 0.15
CHUNK = 8
PIECE = 2
HALF = CHUNK // 2
BANDS = 2
HALO = 3
MESH = pl.DeviceIdType.MESH
F32 = jnp.float32
BF16 = jnp.bfloat16


def dft_tables(length):
    index = np.arange(length)
    angle = (index[:, None] * index[None, :] % length) * (2.0 * np.pi / length)
    c = np.cos(angle).astype(np.float32)
    s = np.sin(angle).astype(np.float32)
    right = np.concatenate([c, s], axis=1)
    left = np.block([[c, -s], [-s, -c]])
    inner = np.block([[c, s], [-s, c]])
    last = np.concatenate([c, -s], axis=1)
    tables = np.concatenate([right, left, inner, last], axis=0)
    return jnp.asarray(tables.astype(jnp.bfloat16))


def dot(a, b):
    return jnp.dot(a, b, preferred_element_type=F32)


def dot_nt(a, b):
    return lax.dot_general(a, b, (((1,), (1,)), ((), ())), preferred_element_type=F32)


def split3(x):
    top = x.astype(BF16)
    rest = x - top.astype(F32)
    mid = rest.astype(BF16)
    return top, mid, (rest - mid.astype(F32)).astype(BF16)


def stacked(both, a, b, side):
    ra = both[a * side : (a + 1) * side]
    rb = both[b * side : (b + 1) * side]
    top = jnp.concatenate([ra[:, :side], rb[:, :side]], axis=1)
    low = jnp.concatenate([ra[:, side:], rb[:, side:]], axis=1)
    return jnp.concatenate([top, low], axis=0)


def spectra(images, right, left):
    side = images[0].shape[0]
    rows = jnp.concatenate(images, axis=0)
    both = dot(rows, right).astype(BF16)
    return [dot(left, stacked(both, 2 * i, 2 * i + 1, side)) for i in range(len(images) // 2)]


def lane_roll(x, shift):
    return pltpu.roll(x, shift % x.shape[-1], x.ndim - 1)


def single(pair):
    return pair % 2


def up_tail(up):
    return jnp.minimum(jnp.maximum(up - 1, 0), 1)


def down_tail(up, chunks):
    return jnp.minimum(chunks - 1 - up, 1)


def up_chunks(pair, n, chunks):
    return chunks * ((pair + 1) // 2) // (n // 2)


def exchange(
    n,
    tables_any,
    list_any,
    count_s,
    tissue_any,
    patches_any,
    out_ref,
    patches_a,
    patches_b,
    tables,
    list_v,
    list_s,
    tissue_v,
    note,
    far_note,
    far_s,
    outgoing,
    incoming,
    own_spec,
    peak_ref,
    mass_ref,
    moment_ref,
    packet,
    halo,
    load_sems,
    list_sems,
    send_sems,
    recv_sems,
    halo_send,
    halo_recv,
    near_sem,
    far_sem,
):
    me = lax.axis_index("sec")
    patches = (patches_a, patches_b)
    total, _, side = patches_a.shape
    slots = list_v.shape[1]
    chunks = slots // CHUNK
    offsets = [d for d in range(-HALO, HALO + 1) if d != 0]

    loads = [
        pltpu.make_async_copy(source, target, load_sems.at[i])
        for i, (source, target) in enumerate(
            (
                (list_any, list_s),
                (list_any, list_v),
                (tables_any, tables),
                (tissue_any, tissue_v),
            )
        )
    ]
    loads[0].start()
    loads[1].start()
    bands = [pl.ds(i * side // BANDS, side // BANDS) for i in range(BANDS)]
    band_loads = [
        pltpu.make_async_copy(
            patches_any.at[0, :, band], patches[i], load_sems.at[4 + i]
        )
        for i, band in enumerate(bands)
    ]
    for load in band_loads:
        load.start()
    loads[2].start()
    loads[3].start()

    halo[...] = jnp.zeros_like(halo)
    far_note[...] = jnp.zeros_like(far_note)

    barrier = pltpu.get_barrier_semaphore()

    def greet(sem):
        for to in (me + 1 - 2 * (me % 2), me - 1 + 2 * (me % 2)):

            @pl.when((to >= 0) & (to < n))
            def _():
                pl.semaphore_signal(sem, inc=1, device_id={"sec": to}, device_id_type=MESH)

    greet(barrier)

    peak_ref[...] = jnp.zeros_like(peak_ref)
    mass_ref[...] = jnp.ones_like(mass_ref)
    moment_ref[...] = jnp.zeros_like(moment_ref)
    loads[0].wait()
    loads[1].wait()
    count = count_s[0]
    note[...] = jnp.concatenate([list_v[...], jnp.full((1, slots), count, jnp.int32)], axis=0)

    has_up = jnp.minimum(n - 1 - me, 1)
    has_down = jnp.minimum(me, 1)
    my_up = up_chunks(me, n, chunks)
    far_up = up_chunks(me - 1, n, chunks)
    my_odd, far_odd = has_up * (me % 2), has_down * (1 - me % 2)
    up_tail_to, up_tail_in = my_odd * up_tail(my_up), far_odd * up_tail(far_up)
    down_tail_in, down_tail_to = my_odd * down_tail(my_up, chunks), far_odd * down_tail(far_up, chunks)
    tail_in = up_tail_in + down_tail_in
    my_half = has_up * single(me)
    far_half = has_down * single(me - 1)

    sides = jnp.minimum(me, 1) + jnp.minimum(n - 1 - me, 1)
    pl.semaphore_wait(barrier, sides)

    list_copy = pltpu.make_async_remote_copy(
        src_ref=note,
        dst_ref=far_note,
        send_sem=list_sems.at[0],
        recv_sem=list_sems.at[1],
        device_id={"sec": me + 1},
        device_id_type=MESH,
    )

    slot_copy = pltpu.make_async_remote_copy(
        src_ref=list_v,
        dst_ref=far_s,
        send_sem=list_sems.at[2],
        recv_sem=list_sems.at[3],
        device_id={"sec": me + 1},
        device_id_type=MESH,
    )

    @pl.when(me < n - 1)
    def _():
        slot_copy.start()
        list_copy.start()


    def patch_copy(q, to):
        return pltpu.make_async_remote_copy(
            src_ref=outgoing.at[pl.ds(q * CHUNK, CHUNK)],
            dst_ref=incoming.at[pl.ds(q * CHUNK, CHUNK)],
            send_sem=send_sems.at[0],
            recv_sem=recv_sems.at[q],
            device_id={"sec": to},
            device_id_type=MESH,
        )

    def half_copy(q, i, to):
        at = pl.ds(q * CHUNK + i * HALF, HALF)
        return pltpu.make_async_remote_copy(
            src_ref=outgoing.at[at],
            dst_ref=incoming.at[at],
            send_sem=send_sems.at[0],
            recv_sem=recv_sems.at[2 * chunks + i],
            device_id={"sec": to},
            device_id_type=MESH,
        )

    def piece_copy(q, first, size, to):
        at = pl.ds(q * CHUNK + first, size)
        return pltpu.make_async_remote_copy(
            src_ref=outgoing.at[at],
            dst_ref=incoming.at[at],
            send_sem=send_sems.at[0],
            recv_sem=recv_sems.at[q],
            device_id={"sec": to},
            device_id_type=MESH,
        )

    def gather(source, q, c, first, count):
        for j in range(first, first + count):
            for part, band in zip(patches, bands):
                outgoing[q * CHUNK + j, band] = part[source[0, c * CHUNK + j]]

    def send_up(c, carry):
        gather(list_s, c, c, 0, CHUNK)
        patch_copy(c, me + 1).start()
        return carry

    for i, band in enumerate(bands):
        band_loads[i].wait()

        @pl.when(has_up * my_up > 0)
        def _():
            for j in range(CHUNK):
                outgoing[j, band] = patches[i][list_s[0, j]]
            pltpu.make_async_remote_copy(
                src_ref=outgoing.at[0:CHUNK, band],
                dst_ref=incoming.at[0:CHUNK, band],
                send_sem=send_sems.at[0],
                recv_sem=recv_sems.at[0],
                device_id={"sec": me + 1},
                device_id_type=MESH,
            ).start()

    n_up = has_up * my_up - up_tail_to
    lax.fori_loop(1, n_up, send_up, 0)

    @pl.when(my_half > 0)
    def _():
        gather(list_s, my_up, my_up, 0, PIECE)
        piece_copy(my_up, 0, PIECE, me + 1).start()

    @pl.when(up_tail_to > 0)
    def _():
        for i in range(2):
            gather(list_s, my_up - 1, my_up - 1, i * HALF, HALF)
            half_copy(my_up - 1, i, me + 1).start()

    greet(near_sem)
    right_ref = tables.at[0:side]
    left_ref = tables.at[side : 3 * side]
    inner_ref = tables.at[3 * side : 5 * side]
    last_ref = tables.at[5 * side : 6 * side]

    def own_group(q, carry):
        images = []
        for j in range(CHUNK):
            far = far_s[0, jnp.minimum(q, chunks - 1) * CHUNK + j]
            near = list_s[0, jnp.maximum(q - chunks, 0) * CHUNK + j]
            at = jnp.where(q < chunks, far, near)
            images.append(jnp.concatenate([part[at] for part in patches], axis=0))
        for i, spec in enumerate(spectra(images, right_ref[...], left_ref[...])):
            own_spec[q * (CHUNK // 2) + i] = spec.astype(BF16)
        return carry

    @pl.when(me > 0)
    def _():
        slot_copy.wait_recv()

    @pl.when(me == 0)
    def _():
        fill = pltpu.make_async_copy(list_v, far_s, list_sems.at[3])
        fill.start()
        fill.wait()

    @pl.when(far_half > 0)
    def _():
        gather(far_s, chunks + far_up, far_up, PIECE, CHUNK - PIECE)
        piece_copy(chunks + far_up, PIECE, CHUNK - PIECE, me - 1).start()

    down_from = far_up + far_half

    def send_down(c, carry):
        gather(far_s, chunks + c, c, 0, CHUNK)
        patch_copy(chunks + c, me - 1).start()
        return carry

    n_down = has_down * (chunks - down_from) - down_tail_to
    lax.fori_loop(down_from, down_from + n_down, send_down, 0)

    @pl.when(down_tail_to > 0)
    def _():
        for i in range(2):
            gather(far_s, 2 * chunks - 1, chunks - 1, i * HALF, HALF)
            half_copy(2 * chunks - 1, i, me - 1).start()

    for load in loads[2:]:
        load.wait()
    lax.fori_loop(chunks + my_up, chunks + my_up + has_up * (chunks - my_up), own_group, 0)
    lax.fori_loop(0, has_down * far_up + far_half, own_group, 0)

    pl.semaphore_wait(near_sem, sides)
    greet(far_sem)
    @pl.when(me > 0)
    def _():
        list_copy.wait_recv()

    half = side // 2
    row = lax.broadcasted_iota(jnp.int32, (side, 1), 0)
    row_lag = ((row + half) % side - half).astype(F32)
    scale = 64.0 / float(side * side * side * side)

    def match(slot, size):
        sign = jnp.where(slot < slots, -1.0, 1.0).astype(F32)
        images = [incoming[slot + j] for j in range(size)]
        crosses = []
        for i, spec in enumerate(spectra(images, right_ref[...], left_ref[...])):
            ar = spec[:side].astype(BF16).astype(F32)
            ai = spec[side:].astype(BF16).astype(F32)
            own = own_spec[slot // 2 + i].astype(F32)
            br, bi = own[:side], own[side:]
            cr = (br * ar + bi * ai).astype(BF16)
            ci = ((br * ai - bi * ar) * sign).astype(BF16)
            crosses.append(jnp.concatenate([cr[:, :side], ci[:, :side]], axis=1))
            crosses.append(jnp.concatenate([cr[:, side:], ci[:, side:]], axis=1))
        inner = dot(jnp.concatenate(crosses, axis=0), inner_ref[...]).astype(BF16)
        peaks, masses, moments = [], [], []
        for i in range(size // 2):
            scores = dot(last_ref[...], stacked(inner, 2 * i, 2 * i + 1, side)) * scale
            peak = jnp.max(scores, axis=0, keepdims=True)
            e = jnp.exp(scores - peak)
            mass = jnp.sum(e, axis=0, keepdims=True)
            moment = jnp.sum(e * row_lag, axis=0, keepdims=True)
            for parts, value in ((peaks, peak), (masses, mass), (moments, moment)):
                parts.append(value[:, :side])
                parts.append(value[:, side:])
        return [jnp.concatenate(parts, axis=0) for parts in (peaks, masses, moments)]

    def match_group(t, carry):
        start_a, count_a, start_b = carry
        q = jnp.where(t < count_a, start_a + t, start_b + t - count_a)
        skip = up_tail_in * (q < chunks).astype(jnp.int32) * (q >= far_up - 1).astype(jnp.int32)
        q = q + skip
        is_far_half = (q == far_up) & (far_half > 0)
        is_my_half = (q == chunks + my_up) & (my_half > 0)

        @pl.when(is_far_half)
        def _():
            piece_copy(q, 0, PIECE, me).wait_recv()

        @pl.when(is_my_half)
        def _():
            piece_copy(q, PIECE, CHUNK - PIECE, me).wait_recv()

        @pl.when(jnp.logical_not(is_far_half | is_my_half))
        def _():
            patch_copy(q, me).wait_recv()

        slot = pl.multiple_of(q * CHUNK, CHUNK)
        peaks, masses, moments = match(slot, CHUNK)
        at = pl.ds(slot, CHUNK)
        peak_ref[at, :] = peaks
        mass_ref[at, :] = masses
        moment_ref[at, :] = moments
        return carry

    n_far = has_down * far_up + far_half
    n_near = has_up * (chunks - my_up)
    odd = me % 2
    start_a = (1 - odd) * (chunks + my_up)
    start_b = odd * (chunks + my_up)
    count_a = odd * n_far + (1 - odd) * n_near
    tail_q = jnp.where(up_tail_in > 0, far_up - 1, 2 * chunks - 1)
    n_main = n_far + n_near - tail_in
    lax.fori_loop(0, n_main, match_group, (start_a, count_a, start_b))

    peak = peak_ref[...]
    weight = jnp.exp(peak - jnp.max(peak, axis=1, keepdims=True))
    mass = mass_ref[...] * weight
    moment = moment_ref[...] * weight
    col = lax.broadcasted_iota(jnp.int32, (8, side), 1)
    sub = lax.broadcasted_iota(jnp.int32, (8, side), 0)
    col_lag = ((col + half) % side - half).astype(F32)
    axes = jnp.where(sub == 0, 1.0, jnp.where(sub == 1, col_lag, 0.0))
    thirds = jnp.concatenate(split3(jnp.concatenate([mass, moment], axis=0)), axis=0)
    triple = dot_nt(axes.astype(BF16), thirds)
    span = 4 * slots
    joined = triple[:, 0:span] + triple[:, span : 2 * span] + triple[:, 2 * span :]
    sums, rows_num = joined[:, 0 : 2 * slots], joined[:, 2 * slots :]
    mass_all = sums[0:1]
    place = lax.broadcasted_iota(jnp.int32, (1, 2 * slots), 1)
    is_far = place < slots
    far = far_note[...]
    counts = jnp.concatenate([far[1:2], jnp.full((1, slots), count, jnp.int32)], axis=1)
    lists = jnp.concatenate([far[0:1], list_v[...]], axis=1)
    slot = jnp.where(is_far, place, place - slots)
    first = jnp.where(is_far, 0, (chunks - n_near) * CHUNK + my_half * PIECE)
    stop = jnp.minimum(jnp.where(is_far, n_far * CHUNK - far_half * (CHUNK - PIECE), slots), counts)
    late = (place >= tail_q * CHUNK) & (place < tail_q * CHUNK + CHUNK) & (tail_in > 0)
    live = (slot >= first) & (slot < stop) & jnp.logical_not(late)
    flow_rows = jnp.where(live, rows_num[0:1] / mass_all, 0.0)
    flow_cols = jnp.where(live, sums[1:2] / mass_all, 0.0)
    which = lax.broadcasted_iota(jnp.int32, (total, 2 * slots), 0)
    onehot = (which == lists).astype(F32).astype(BF16)
    one_pair = jnp.concatenate(
        [flow_rows, flow_cols, live.astype(F32), jnp.zeros((5, 2 * slots), F32)], axis=0
    )
    both = jnp.concatenate(
        [jnp.where(is_far, one_pair, 0.0), jnp.where(is_far, 0.0, one_pair)], axis=0
    )
    triple = dot_nt(jnp.concatenate(split3(both), axis=0), onehot)
    field = triple[0:16] + triple[16:32] + triple[32:48]
    packet[0:3] = field[0:3]
    packet[3:4] = tissue_v[...].astype(F32)
    packet[4:8] = field[4:8]
    packet[8:16] = field[8:16]
    packet[4:5, 0 : 2 * slots] = flow_rows
    packet[5:6, 0 : 2 * slots] = flow_cols

    lane = lax.broadcasted_iota(jnp.int32, (HALF, side), 1)
    step = lax.broadcasted_iota(jnp.int32, (HALF, side), 0)
    late_lag = ((lane + half) % side - half).astype(F32)
    spot = lax.broadcasted_iota(jnp.int32, (HALF, total), 1)
    turn = lax.broadcasted_iota(jnp.int32, (HALF, total), 0)
    late_far = up_tail_in > 0
    late_count = jnp.where(late_far, far_note[1:2, 0:1], jnp.full((1, 1), count, jnp.int32))

    def match_tail(i, carry):
        for k in range(2):

            @pl.when(i == k)
            def _():
                half_copy(tail_q, k, me).wait_recv()

        at = pl.multiple_of(tail_q * CHUNK + i * HALF, HALF)
        peak, mass, moment = match(at, HALF)
        weight = jnp.exp(peak - jnp.max(peak, axis=1, keepdims=True))
        mass = mass * weight
        whole = jnp.sum(mass, axis=1, keepdims=True)
        rows = jnp.sum(moment * weight, axis=1, keepdims=True) / whole
        cols = jnp.sum(mass * late_lag, axis=1, keepdims=True) / whole
        own_at = jnp.where(late_far, at, at - slots)
        ids = jnp.zeros((HALF, total), jnp.int32)
        for j in range(HALF):
            listed = jnp.where(late_far, far_s[0, own_at + j], list_s[0, own_at + j])
            ids = jnp.where(turn == j, listed, ids)
        alive = turn + own_at < late_count
        hit = (spot == ids) & alive
        here = (spot == turn + at) & alive
        picks = [
            jnp.where(hit, rows, 0.0),
            jnp.where(hit, cols, 0.0),
            hit.astype(F32),
            jnp.where(here, rows, 0.0),
            jnp.where(here, cols, 0.0),
        ]
        picks = [jnp.sum(pick, axis=0, keepdims=True) for pick in picks]
        extra = jnp.concatenate(picks[:3], axis=0)
        packet[0:3] = packet[0:3] + jnp.where(late_far, extra, 0.0)
        packet[8:11] = packet[8:11] + jnp.where(late_far, 0.0, extra)
        packet[4:6] = packet[4:6] + jnp.concatenate(picks[3:], axis=0)
        return carry

    lax.fori_loop(0, 2 * tail_in, match_tail, 0)

    pl.semaphore_wait(far_sem, sides)

    def halo_copy(d):
        return pltpu.make_async_remote_copy(
            src_ref=packet,
            dst_ref=halo.at[HALO - d],
            send_sem=halo_send.at[0],
            recv_sem=halo_recv.at[HALO - d],
            device_id={"sec": me + d},
            device_id_type=MESH,
        )

    for d in offsets:

        @pl.when((me + d >= 0) & (me + d < n))
        def _():
            halo_copy(d).start()

    @pl.when(me < n - 1)
    def _():
        slot_copy.wait_send()
        list_copy.wait_send()

    def drain_up(c, carry):
        patch_copy(c, me + 1).wait_send()
        return carry

    lax.fori_loop(0, n_up, drain_up, 0)

    @pl.when(up_tail_to > 0)
    def _():
        for i in range(2):
            half_copy(my_up - 1, i, me + 1).wait_send()

    @pl.when(my_half > 0)
    def _():
        piece_copy(my_up, 0, PIECE, me + 1).wait_send()

    def drain_down(c, carry):
        patch_copy(chunks + c, me - 1).wait_send()
        return carry

    lax.fori_loop(down_from, down_from + n_down, drain_down, 0)

    @pl.when(down_tail_to > 0)
    def _():
        for i in range(2):
            half_copy(2 * chunks - 1, i, me - 1).wait_send()

    @pl.when(far_half > 0)
    def _():
        piece_copy(chunks + far_up, PIECE, CHUNK - PIECE, me - 1).wait_send()

    for d in offsets:

        @pl.when((me - d >= 0) & (me - d < n))
        def _():
            halo_copy(d).wait_recv()

    halo[HALO] = packet[...]
    relax(slots, halo, out_ref)
    for d in offsets:

        @pl.when((me + d >= 0) & (me + d < n))
        def _():
            halo_copy(d).wait_send()


def relax(slots, halo, out_ref):
    total = halo.shape[-1]
    near, above = halo[HALO], halo[HALO + 1]
    out_ref[2:4, 0:slots] = near[4:6, slots : 2 * slots] + above[4:6, 0:slots]
    fields = {d: halo[HALO + d][8:16] + halo[HALO + d + 1][0:8] for d in range(-HALO, HALO)}
    links = {d: jnp.broadcast_to(f[2:3], f.shape) for d, f in fields.items()}
    lane = lax.broadcasted_iota(jnp.int32, (8, total), 1)
    width = total // GR
    has_right = (lane % width) != width - 1
    has_below = lane < total - width

    def springs(d):
        tissue = jnp.broadcast_to(halo[HALO + d][3:4], (8, total))
        stiff = SPRING * (1.0 + 2.0 * tissue)
        across = jnp.where(has_right, 0.5 * (stiff + lane_roll(stiff, -1)), 0.0)
        along = jnp.where(has_below, 0.5 * (stiff + lane_roll(stiff, -width)), 0.0)
        return across, along

    def plane(u, spring):
        across, along = spring
        a = across * (lane_roll(u, -1) - u)
        b = along * (lane_roll(u, -width) - u)
        return (lane_roll(a, 1) - a) + (lane_roll(b, width) - b)

    spring = {d: springs(d) for d in (-1, 0, 1)}
    pull = {d: links[d] * fields[d] for d in fields}
    u1 = {d: -STEP * (pull[d] - pull[d - 1]) for d in range(-2, 3)}

    def relaxed(u, d):
        gap_here = u[d + 1] - u[d] - fields[d]
        gap_below = u[d] - u[d - 1] - fields[d - 1]
        force = plane(u[d], spring[d]) - links[d] * gap_here + links[d - 1] * gap_below
        return u[d] - STEP * force

    u2 = {d: relaxed(u1, d) for d in (-1, 0, 1)}
    out_ref[0:2] = relaxed(u2, 0)[0:2]


def unpack(both, flow_ref, pos_ref):
    flow_ref[0] = both[2:4, 0 : flow_ref.shape[-1]]
    pos_ref[0] = both[0:2]


def on_device(n, patches, pair_list, pair_count, tissue):
    _, total, side, _ = patches.shape
    slots = pair_list.shape[1]
    chunks = slots // CHUNK
    vmem = pl.BlockSpec(memory_space=pltpu.VMEM)
    any_space = pl.BlockSpec(memory_space=pl.ANY)
    dma = pltpu.SemaphoreType.DMA
    both = pl.pallas_call(
        functools.partial(exchange, n),
        out_shape=pltpu.VMEM((4, total), F32),
        in_specs=[any_space] * 2 + [pl.BlockSpec(memory_space=pltpu.SMEM)] + [any_space] * 2,
        out_specs=vmem,
        scratch_shapes=[
            pltpu.VMEM((total, side // BANDS, side), BF16),
            pltpu.VMEM((total, side // BANDS, side), BF16),
            pltpu.VMEM((6 * side, 2 * side), BF16),
            pltpu.VMEM((1, slots), jnp.int32),
            pltpu.SMEM((1, slots), jnp.int32),
            pltpu.VMEM((1, total), jnp.int32),
            pltpu.VMEM((2, slots), jnp.int32),
            pltpu.VMEM((2, slots), jnp.int32),
            pltpu.SMEM((1, slots), jnp.int32),
            pltpu.VMEM((2 * slots, side, side), BF16),
            pltpu.VMEM((2 * slots, side, side), BF16),
            pltpu.VMEM((slots, 2 * side, 2 * side), BF16),
            pltpu.VMEM((2 * slots, side), F32),
            pltpu.VMEM((2 * slots, side), F32),
            pltpu.VMEM((2 * slots, side), F32),
            pltpu.VMEM((16, total), F32),
            pltpu.VMEM((2 * HALO + 1, 16, total), F32),
            dma((4 + BANDS,)),
            dma((4,)),
            dma((1,)),
            dma((2 * chunks + 2,)),
            dma((1,)),
            dma((2 * HALO + 1,)),
            pltpu.SemaphoreType.REGULAR,
            pltpu.SemaphoreType.REGULAR,
        ],
        compiler_params=pltpu.CompilerParams(
            collective_id=0, has_side_effects=True, vmem_limit_bytes=64_000_000
        ),
        name="exchange",
    )(dft_tables(side), pair_list, pair_count, tissue, patches)
    return pl.pallas_call(
        unpack,
        out_shape=(
            jax.ShapeDtypeStruct((1, 2, slots), F32),
            jax.ShapeDtypeStruct((1, 2, total), F32),
        ),
        in_specs=[vmem],
        out_specs=(vmem, vmem),
        compiler_params=pltpu.CompilerParams(vmem_limit_bytes=2_000_000),
        name="unpack",
    )(both)


def solution(mesh):
    return jax.shard_map(
        functools.partial(on_device, mesh.shape["sec"]),
        mesh=mesh,
        in_specs=(
            P(("group", "sec"), None, None, None),
            P(("group", "sec"), None),
            P(("group", "sec")),
            P(("group", "sec"), None),
        ),
        out_specs=(P(("group", "sec"), None, None), P(("group", "sec"), None, None)),
        check_vma=False,
    )
```

```python
import functools

import jax
import jax.numpy as jnp
import numpy as np
from jax import lax
from jax.experimental import pallas as pl
from jax.experimental.pallas import tpu as pltpu
from jax.sharding import PartitionSpec as P

GR = 8
SPRING = 0.25
STEP = 0.15
CHUNK = 8
PIECES = (1, 2, 3)
HALF = CHUNK // 2
BANDS = 2
HALO = 3
MESH = pl.DeviceIdType.MESH
F32 = jnp.float32
BF16 = jnp.bfloat16


def dft_tables(length):
    index = np.arange(length)
    angle = (index[:, None] * index[None, :] % length) * (2.0 * np.pi / length)
    c = np.cos(angle).astype(np.float32)
    s = np.sin(angle).astype(np.float32)
    right = np.concatenate([c, s], axis=1)
    left = np.block([[c, -s], [-s, -c]])
    inner = np.block([[c, s], [-s, c]])
    last = np.concatenate([c, -s], axis=1)
    tables = np.concatenate([right, left, inner, last], axis=0)
    return jnp.asarray(tables.astype(jnp.bfloat16))


def dot(a, b):
    return jnp.dot(a, b, preferred_element_type=F32)


def dot_nt(a, b):
    return lax.dot_general(a, b, (((1,), (1,)), ((), ())), preferred_element_type=F32)


def split3(x):
    top = x.astype(BF16)
    rest = x - top.astype(F32)
    mid = rest.astype(BF16)
    return top, mid, (rest - mid.astype(F32)).astype(BF16)


def stacked(both, a, b, side):
    ra = both[a * side : (a + 1) * side]
    rb = both[b * side : (b + 1) * side]
    top = jnp.concatenate([ra[:, :side], rb[:, :side]], axis=1)
    low = jnp.concatenate([ra[:, side:], rb[:, side:]], axis=1)
    return jnp.concatenate([top, low], axis=0)


def spectra(images, right, left):
    side = images[0].shape[0]
    rows = jnp.concatenate(images, axis=0)
    both = dot(rows, right).astype(BF16)
    return [dot(left, stacked(both, 2 * i, 2 * i + 1, side)) for i in range(len(images) // 2)]


def lane_roll(x, shift):
    return pltpu.roll(x, shift % x.shape[-1], x.ndim - 1)


def piece_of(pair, n):
    spot, middle = (pair + 1) // 2, n // 4
    size = 1 + jnp.minimum(jnp.maximum(middle + 1 - spot, 0), 2)
    return (pair % 2) * size


def up_tail(up):
    return jnp.minimum(jnp.maximum(up - 1, 0), 1)


def down_tail(up, chunks):
    return jnp.minimum(chunks - 1 - up, 1)


def up_chunks(pair, n, chunks):
    return chunks * ((pair + 1) // 2) // (n // 2)


def exchange(
    n,
    tables_any,
    list_any,
    count_s,
    tissue_any,
    patches_any,
    out_ref,
    patches_a,
    patches_b,
    tables,
    list_v,
    list_s,
    tissue_v,
    note,
    far_note,
    far_s,
    outgoing,
    incoming,
    own_spec,
    peak_ref,
    mass_ref,
    moment_ref,
    packet,
    halo,
    load_sems,
    list_sems,
    send_sems,
    recv_sems,
    halo_send,
    halo_recv,
    near_sem,
    far_sem,
):
    me = lax.axis_index("sec")
    patches = (patches_a, patches_b)
    total, _, side = patches_a.shape
    slots = list_v.shape[1]
    chunks = slots // CHUNK
    offsets = [d for d in range(-HALO, HALO + 1) if d != 0]

    loads = [
        pltpu.make_async_copy(source, target, load_sems.at[i])
        for i, (source, target) in enumerate(
            (
                (list_any, list_s),
                (list_any, list_v),
                (tables_any, tables),
                (tissue_any, tissue_v),
            )
        )
    ]
    loads[0].start()
    loads[1].start()
    bands = [pl.ds(i * side // BANDS, side // BANDS) for i in range(BANDS)]
    band_loads = [
        pltpu.make_async_copy(
            patches_any.at[0, :, band], patches[i], load_sems.at[4 + i]
        )
        for i, band in enumerate(bands)
    ]
    for load in band_loads:
        load.start()
    loads[2].start()
    loads[3].start()

    halo[...] = jnp.zeros_like(halo)
    far_note[...] = jnp.zeros_like(far_note)

    barrier = pltpu.get_barrier_semaphore()

    def greet(sem):
        for to in (me + 1 - 2 * (me % 2), me - 1 + 2 * (me % 2)):

            @pl.when((to >= 0) & (to < n))
            def _():
                pl.semaphore_signal(sem, inc=1, device_id={"sec": to}, device_id_type=MESH)

    greet(barrier)

    peak_ref[...] = jnp.zeros_like(peak_ref)
    mass_ref[...] = jnp.ones_like(mass_ref)
    moment_ref[...] = jnp.zeros_like(moment_ref)
    loads[0].wait()
    loads[1].wait()
    count = count_s[0]
    note[...] = jnp.concatenate([list_v[...], jnp.full((1, slots), count, jnp.int32)], axis=0)

    has_up = jnp.minimum(n - 1 - me, 1)
    has_down = jnp.minimum(me, 1)
    my_up = up_chunks(me, n, chunks)
    far_up = up_chunks(me - 1, n, chunks)
    my_odd, far_odd = has_up * (me % 2), has_down * (1 - me % 2)
    up_tail_to, up_tail_in = my_odd * up_tail(my_up), far_odd * up_tail(far_up)
    down_tail_in, down_tail_to = my_odd * down_tail(my_up, chunks), far_odd * down_tail(far_up, chunks)
    tail_in = up_tail_in + down_tail_in
    my_piece = has_up * piece_of(me, n)
    far_piece = has_down * piece_of(me - 1, n)
    my_half, far_half = jnp.minimum(my_piece, 1), jnp.minimum(far_piece, 1)

    sides = jnp.minimum(me, 1) + jnp.minimum(n - 1 - me, 1)
    pl.semaphore_wait(barrier, sides)

    list_copy = pltpu.make_async_remote_copy(
        src_ref=note,
        dst_ref=far_note,
        send_sem=list_sems.at[0],
        recv_sem=list_sems.at[1],
        device_id={"sec": me + 1},
        device_id_type=MESH,
    )

    slot_copy = pltpu.make_async_remote_copy(
        src_ref=list_v,
        dst_ref=far_s,
        send_sem=list_sems.at[2],
        recv_sem=list_sems.at[3],
        device_id={"sec": me + 1},
        device_id_type=MESH,
    )

    @pl.when(me < n - 1)
    def _():
        slot_copy.start()
        list_copy.start()


    def patch_copy(q, to):
        return pltpu.make_async_remote_copy(
            src_ref=outgoing.at[pl.ds(q * CHUNK, CHUNK)],
            dst_ref=incoming.at[pl.ds(q * CHUNK, CHUNK)],
            send_sem=send_sems.at[0],
            recv_sem=recv_sems.at[q],
            device_id={"sec": to},
            device_id_type=MESH,
        )

    def half_copy(q, i, to):
        at = pl.ds(q * CHUNK + i * HALF, HALF)
        return pltpu.make_async_remote_copy(
            src_ref=outgoing.at[at],
            dst_ref=incoming.at[at],
            send_sem=send_sems.at[0],
            recv_sem=recv_sems.at[2 * chunks + i],
            device_id={"sec": to},
            device_id_type=MESH,
        )

    def piece_copy(q, first, size, to):
        at = pl.ds(q * CHUNK + first, size)
        return pltpu.make_async_remote_copy(
            src_ref=outgoing.at[at],
            dst_ref=incoming.at[at],
            send_sem=send_sems.at[0],
            recv_sem=recv_sems.at[q],
            device_id={"sec": to},
            device_id_type=MESH,
        )

    def gather(source, q, c, first, count):
        for j in range(first, first + count):
            for part, band in zip(patches, bands):
                outgoing[q * CHUNK + j, band] = part[source[0, c * CHUNK + j]]

    def send_up(c, carry):
        gather(list_s, c, c, 0, CHUNK)
        patch_copy(c, me + 1).start()
        return carry

    for i, band in enumerate(bands):
        band_loads[i].wait()

        @pl.when(has_up * my_up > 0)
        def _():
            for j in range(CHUNK):
                outgoing[j, band] = patches[i][list_s[0, j]]
            pltpu.make_async_remote_copy(
                src_ref=outgoing.at[0:CHUNK, band],
                dst_ref=incoming.at[0:CHUNK, band],
                send_sem=send_sems.at[0],
                recv_sem=recv_sems.at[0],
                device_id={"sec": me + 1},
                device_id_type=MESH,
            ).start()

    n_up = has_up * my_up - up_tail_to
    lax.fori_loop(1, n_up, send_up, 0)

    for size in PIECES:

        @pl.when(my_piece == size)
        def _():
            gather(list_s, my_up, my_up, 0, size)
            piece_copy(my_up, 0, size, me + 1).start()

    @pl.when(up_tail_to > 0)
    def _():
        for i in range(2):
            gather(list_s, my_up - 1, my_up - 1, i * HALF, HALF)
            half_copy(my_up - 1, i, me + 1).start()

    greet(near_sem)
    right_ref = tables.at[0:side]
    left_ref = tables.at[side : 3 * side]
    inner_ref = tables.at[3 * side : 5 * side]
    last_ref = tables.at[5 * side : 6 * side]

    def own_group(q, carry):
        images = []
        for j in range(CHUNK):
            far = far_s[0, jnp.minimum(q, chunks - 1) * CHUNK + j]
            near = list_s[0, jnp.maximum(q - chunks, 0) * CHUNK + j]
            at = jnp.where(q < chunks, far, near)
            images.append(jnp.concatenate([part[at] for part in patches], axis=0))
        for i, spec in enumerate(spectra(images, right_ref[...], left_ref[...])):
            own_spec[q * (CHUNK // 2) + i] = spec.astype(BF16)
        return carry

    @pl.when(me > 0)
    def _():
        slot_copy.wait_recv()

    @pl.when(me == 0)
    def _():
        fill = pltpu.make_async_copy(list_v, far_s, list_sems.at[3])
        fill.start()
        fill.wait()

    for size in PIECES:

        @pl.when(far_piece == size)
        def _():
            gather(far_s, chunks + far_up, far_up, size, CHUNK - size)
            piece_copy(chunks + far_up, size, CHUNK - size, me - 1).start()

    down_from = far_up + far_half

    def send_down(c, carry):
        gather(far_s, chunks + c, c, 0, CHUNK)
        patch_copy(chunks + c, me - 1).start()
        return carry

    n_down = has_down * (chunks - down_from) - down_tail_to
    lax.fori_loop(down_from, down_from + n_down, send_down, 0)

    @pl.when(down_tail_to > 0)
    def _():
        for i in range(2):
            gather(far_s, 2 * chunks - 1, chunks - 1, i * HALF, HALF)
            half_copy(2 * chunks - 1, i, me - 1).start()

    for load in loads[2:]:
        load.wait()
    lax.fori_loop(chunks + my_up, chunks + my_up + has_up * (chunks - my_up), own_group, 0)
    lax.fori_loop(0, has_down * far_up + far_half, own_group, 0)

    pl.semaphore_wait(near_sem, sides)
    greet(far_sem)
    @pl.when(me > 0)
    def _():
        list_copy.wait_recv()

    half = side // 2
    row = lax.broadcasted_iota(jnp.int32, (side, 1), 0)
    row_lag = ((row + half) % side - half).astype(F32)
    scale = 64.0 / float(side * side * side * side)

    def match(slot, size):
        sign = jnp.where(slot < slots, -1.0, 1.0).astype(F32)
        images = [incoming[slot + j] for j in range(size)]
        crosses = []
        for i, spec in enumerate(spectra(images, right_ref[...], left_ref[...])):
            ar = spec[:side].astype(BF16).astype(F32)
            ai = spec[side:].astype(BF16).astype(F32)
            own = own_spec[slot // 2 + i].astype(F32)
            br, bi = own[:side], own[side:]
            cr = (br * ar + bi * ai).astype(BF16)
            ci = ((br * ai - bi * ar) * sign).astype(BF16)
            crosses.append(jnp.concatenate([cr[:, :side], ci[:, :side]], axis=1))
            crosses.append(jnp.concatenate([cr[:, side:], ci[:, side:]], axis=1))
        inner = dot(jnp.concatenate(crosses, axis=0), inner_ref[...]).astype(BF16)
        peaks, masses, moments = [], [], []
        for i in range(size // 2):
            scores = dot(last_ref[...], stacked(inner, 2 * i, 2 * i + 1, side)) * scale
            peak = jnp.max(scores, axis=0, keepdims=True)
            e = jnp.exp(scores - peak)
            mass = jnp.sum(e, axis=0, keepdims=True)
            moment = jnp.sum(e * row_lag, axis=0, keepdims=True)
            for parts, value in ((peaks, peak), (masses, mass), (moments, moment)):
                parts.append(value[:, :side])
                parts.append(value[:, side:])
        return [jnp.concatenate(parts, axis=0) for parts in (peaks, masses, moments)]

    def match_group(t, carry):
        start_a, count_a, start_b = carry
        q = jnp.where(t < count_a, start_a + t, start_b + t - count_a)
        skip = up_tail_in * (q < chunks).astype(jnp.int32) * (q >= far_up - 1).astype(jnp.int32)
        q = q + skip
        is_far_half = (q == far_up) & (far_half > 0)
        is_my_half = (q == chunks + my_up) & (my_half > 0)

        for size in PIECES:

            @pl.when(is_far_half & (far_piece == size))
            def _():
                piece_copy(q, 0, size, me).wait_recv()

            @pl.when(is_my_half & (my_piece == size))
            def _():
                piece_copy(q, size, CHUNK - size, me).wait_recv()

        @pl.when(jnp.logical_not(is_far_half | is_my_half))
        def _():
            patch_copy(q, me).wait_recv()

        slot = pl.multiple_of(q * CHUNK, CHUNK)
        peaks, masses, moments = match(slot, CHUNK)
        at = pl.ds(slot, CHUNK)
        peak_ref[at, :] = peaks
        mass_ref[at, :] = masses
        moment_ref[at, :] = moments
        return carry

    n_far = has_down * far_up + far_half
    n_near = has_up * (chunks - my_up)
    odd = me % 2
    start_a = (1 - odd) * (chunks + my_up)
    start_b = odd * (chunks + my_up)
    count_a = odd * n_far + (1 - odd) * n_near
    tail_q = jnp.where(up_tail_in > 0, far_up - 1, 2 * chunks - 1)
    n_main = n_far + n_near - tail_in
    lax.fori_loop(0, n_main, match_group, (start_a, count_a, start_b))

    peak = peak_ref[...]
    weight = jnp.exp(peak - jnp.max(peak, axis=1, keepdims=True))
    mass = mass_ref[...] * weight
    moment = moment_ref[...] * weight
    col = lax.broadcasted_iota(jnp.int32, (8, side), 1)
    sub = lax.broadcasted_iota(jnp.int32, (8, side), 0)
    col_lag = ((col + half) % side - half).astype(F32)
    axes = jnp.where(sub == 0, 1.0, jnp.where(sub == 1, col_lag, 0.0))
    thirds = jnp.concatenate(split3(jnp.concatenate([mass, moment], axis=0)), axis=0)
    triple = dot_nt(axes.astype(BF16), thirds)
    span = 4 * slots
    joined = triple[:, 0:span] + triple[:, span : 2 * span] + triple[:, 2 * span :]
    sums, rows_num = joined[:, 0 : 2 * slots], joined[:, 2 * slots :]
    mass_all = sums[0:1]
    place = lax.broadcasted_iota(jnp.int32, (1, 2 * slots), 1)
    is_far = place < slots
    far = far_note[...]
    counts = jnp.concatenate([far[1:2], jnp.full((1, slots), count, jnp.int32)], axis=1)
    lists = jnp.concatenate([far[0:1], list_v[...]], axis=1)
    slot = jnp.where(is_far, place, place - slots)
    first = jnp.where(is_far, 0, (chunks - n_near) * CHUNK + my_piece)
    stop = jnp.minimum(jnp.where(is_far, n_far * CHUNK - (CHUNK * far_half - far_piece), slots), counts)
    late = (place >= tail_q * CHUNK) & (place < tail_q * CHUNK + CHUNK) & (tail_in > 0)
    live = (slot >= first) & (slot < stop) & jnp.logical_not(late)
    flow_rows = jnp.where(live, rows_num[0:1] / mass_all, 0.0)
    flow_cols = jnp.where(live, sums[1:2] / mass_all, 0.0)
    which = lax.broadcasted_iota(jnp.int32, (total, 2 * slots), 0)
    onehot = (which == lists).astype(F32).astype(BF16)
    one_pair = jnp.concatenate(
        [flow_rows, flow_cols, live.astype(F32), jnp.zeros((5, 2 * slots), F32)], axis=0
    )
    both = jnp.concatenate(
        [jnp.where(is_far, one_pair, 0.0), jnp.where(is_far, 0.0, one_pair)], axis=0
    )
    triple = dot_nt(jnp.concatenate(split3(both), axis=0), onehot)
    field = triple[0:16] + triple[16:32] + triple[32:48]
    packet[0:3] = field[0:3]
    packet[3:4] = tissue_v[...].astype(F32)
    packet[4:8] = field[4:8]
    packet[8:16] = field[8:16]
    packet[4:5, 0 : 2 * slots] = flow_rows
    packet[5:6, 0 : 2 * slots] = flow_cols

    lane = lax.broadcasted_iota(jnp.int32, (HALF, side), 1)
    step = lax.broadcasted_iota(jnp.int32, (HALF, side), 0)
    late_lag = ((lane + half) % side - half).astype(F32)
    spot = lax.broadcasted_iota(jnp.int32, (HALF, total), 1)
    turn = lax.broadcasted_iota(jnp.int32, (HALF, total), 0)
    late_far = up_tail_in > 0
    late_count = jnp.where(late_far, far_note[1:2, 0:1], jnp.full((1, 1), count, jnp.int32))

    def match_tail(i, carry):
        for k in range(2):

            @pl.when(i == k)
            def _():
                half_copy(tail_q, k, me).wait_recv()

        at = pl.multiple_of(tail_q * CHUNK + i * HALF, HALF)
        peak, mass, moment = match(at, HALF)
        weight = jnp.exp(peak - jnp.max(peak, axis=1, keepdims=True))
        mass = mass * weight
        whole = jnp.sum(mass, axis=1, keepdims=True)
        rows = jnp.sum(moment * weight, axis=1, keepdims=True) / whole
        cols = jnp.sum(mass * late_lag, axis=1, keepdims=True) / whole
        own_at = jnp.where(late_far, at, at - slots)
        ids = jnp.zeros((HALF, total), jnp.int32)
        for j in range(HALF):
            listed = jnp.where(late_far, far_s[0, own_at + j], list_s[0, own_at + j])
            ids = jnp.where(turn == j, listed, ids)
        alive = turn + own_at < late_count
        hit = (spot == ids) & alive
        here = (spot == turn + at) & alive
        picks = [
            jnp.where(hit, rows, 0.0),
            jnp.where(hit, cols, 0.0),
            hit.astype(F32),
            jnp.where(here, rows, 0.0),
            jnp.where(here, cols, 0.0),
        ]
        picks = [jnp.sum(pick, axis=0, keepdims=True) for pick in picks]
        extra = jnp.concatenate(picks[:3], axis=0)
        packet[0:3] = packet[0:3] + jnp.where(late_far, extra, 0.0)
        packet[8:11] = packet[8:11] + jnp.where(late_far, 0.0, extra)
        packet[4:6] = packet[4:6] + jnp.concatenate(picks[3:], axis=0)
        return carry

    lax.fori_loop(0, 2 * tail_in, match_tail, 0)

    pl.semaphore_wait(far_sem, sides)

    def halo_copy(d):
        return pltpu.make_async_remote_copy(
            src_ref=packet,
            dst_ref=halo.at[HALO - d],
            send_sem=halo_send.at[0],
            recv_sem=halo_recv.at[HALO - d],
            device_id={"sec": me + d},
            device_id_type=MESH,
        )

    for d in offsets:

        @pl.when((me + d >= 0) & (me + d < n))
        def _():
            halo_copy(d).start()

    @pl.when(me < n - 1)
    def _():
        slot_copy.wait_send()
        list_copy.wait_send()

    def drain_up(c, carry):
        patch_copy(c, me + 1).wait_send()
        return carry

    lax.fori_loop(0, n_up, drain_up, 0)

    @pl.when(up_tail_to > 0)
    def _():
        for i in range(2):
            half_copy(my_up - 1, i, me + 1).wait_send()

    for size in PIECES:

        @pl.when(my_piece == size)
        def _():
            piece_copy(my_up, 0, size, me + 1).wait_send()

    def drain_down(c, carry):
        patch_copy(chunks + c, me - 1).wait_send()
        return carry

    lax.fori_loop(down_from, down_from + n_down, drain_down, 0)

    @pl.when(down_tail_to > 0)
    def _():
        for i in range(2):
            half_copy(2 * chunks - 1, i, me - 1).wait_send()

    for size in PIECES:

        @pl.when(far_piece == size)
        def _():
            piece_copy(chunks + far_up, size, CHUNK - size, me - 1).wait_send()

    for d in offsets:

        @pl.when((me - d >= 0) & (me - d < n))
        def _():
            halo_copy(d).wait_recv()

    halo[HALO] = packet[...]
    relax(slots, halo, out_ref)
    for d in offsets:

        @pl.when((me + d >= 0) & (me + d < n))
        def _():
            halo_copy(d).wait_send()


def relax(slots, halo, out_ref):
    total = halo.shape[-1]
    near, above = halo[HALO], halo[HALO + 1]
    out_ref[2:4, 0:slots] = near[4:6, slots : 2 * slots] + above[4:6, 0:slots]
    fields = {d: halo[HALO + d][8:16] + halo[HALO + d + 1][0:8] for d in range(-HALO, HALO)}
    links = {d: jnp.broadcast_to(f[2:3], f.shape) for d, f in fields.items()}
    lane = lax.broadcasted_iota(jnp.int32, (8, total), 1)
    width = total // GR
    has_right = (lane % width) != width - 1
    has_below = lane < total - width

    def springs(d):
        tissue = jnp.broadcast_to(halo[HALO + d][3:4], (8, total))
        stiff = SPRING * (1.0 + 2.0 * tissue)
        across = jnp.where(has_right, 0.5 * (stiff + lane_roll(stiff, -1)), 0.0)
        along = jnp.where(has_below, 0.5 * (stiff + lane_roll(stiff, -width)), 0.0)
        return across, along

    def plane(u, spring):
        across, along = spring
        a = across * (lane_roll(u, -1) - u)
        b = along * (lane_roll(u, -width) - u)
        return (lane_roll(a, 1) - a) + (lane_roll(b, width) - b)

    spring = {d: springs(d) for d in (-1, 0, 1)}
    pull = {d: links[d] * fields[d] for d in fields}
    u1 = {d: -STEP * (pull[d] - pull[d - 1]) for d in range(-2, 3)}

    def relaxed(u, d):
        gap_here = u[d + 1] - u[d] - fields[d]
        gap_below = u[d] - u[d - 1] - fields[d - 1]
        force = plane(u[d], spring[d]) - links[d] * gap_here + links[d - 1] * gap_below
        return u[d] - STEP * force

    u2 = {d: relaxed(u1, d) for d in (-1, 0, 1)}
    out_ref[0:2] = relaxed(u2, 0)[0:2]


def unpack(both, flow_ref, pos_ref):
    flow_ref[0] = both[2:4, 0 : flow_ref.shape[-1]]
    pos_ref[0] = both[0:2]


def on_device(n, patches, pair_list, pair_count, tissue):
    _, total, side, _ = patches.shape
    slots = pair_list.shape[1]
    chunks = slots // CHUNK
    vmem = pl.BlockSpec(memory_space=pltpu.VMEM)
    any_space = pl.BlockSpec(memory_space=pl.ANY)
    dma = pltpu.SemaphoreType.DMA
    both = pl.pallas_call(
        functools.partial(exchange, n),
        out_shape=pltpu.VMEM((4, total), F32),
        in_specs=[any_space] * 2 + [pl.BlockSpec(memory_space=pltpu.SMEM)] + [any_space] * 2,
        out_specs=vmem,
        scratch_shapes=[
            pltpu.VMEM((total, side // BANDS, side), BF16),
            pltpu.VMEM((total, side // BANDS, side), BF16),
            pltpu.VMEM((6 * side, 2 * side), BF16),
            pltpu.VMEM((1, slots), jnp.int32),
            pltpu.SMEM((1, slots), jnp.int32),
            pltpu.VMEM((1, total), jnp.int32),
            pltpu.VMEM((2, slots), jnp.int32),
            pltpu.VMEM((2, slots), jnp.int32),
            pltpu.SMEM((1, slots), jnp.int32),
            pltpu.VMEM((2 * slots, side, side), BF16),
            pltpu.VMEM((2 * slots, side, side), BF16),
            pltpu.VMEM((slots, 2 * side, 2 * side), BF16),
            pltpu.VMEM((2 * slots, side), F32),
            pltpu.VMEM((2 * slots, side), F32),
            pltpu.VMEM((2 * slots, side), F32),
            pltpu.VMEM((16, total), F32),
            pltpu.VMEM((2 * HALO + 1, 16, total), F32),
            dma((4 + BANDS,)),
            dma((4,)),
            dma((1,)),
            dma((2 * chunks + 2,)),
            dma((1,)),
            dma((2 * HALO + 1,)),
            pltpu.SemaphoreType.REGULAR,
            pltpu.SemaphoreType.REGULAR,
        ],
        compiler_params=pltpu.CompilerParams(
            collective_id=0, has_side_effects=True, vmem_limit_bytes=64_000_000
        ),
        name="exchange",
    )(dft_tables(side), pair_list, pair_count, tissue, patches)
    return pl.pallas_call(
        unpack,
        out_shape=(
            jax.ShapeDtypeStruct((1, 2, slots), F32),
            jax.ShapeDtypeStruct((1, 2, total), F32),
        ),
        in_specs=[vmem],
        out_specs=(vmem, vmem),
        compiler_params=pltpu.CompilerParams(vmem_limit_bytes=2_000_000),
        name="unpack",
    )(both)


def solution(mesh):
    return jax.shard_map(
        functools.partial(on_device, mesh.shape["sec"]),
        mesh=mesh,
        in_specs=(
            P(("group", "sec"), None, None, None),
            P(("group", "sec"), None),
            P(("group", "sec")),
            P(("group", "sec"), None),
        ),
        out_specs=(P(("group", "sec"), None, None), P(("group", "sec"), None, None)),
        check_vma=False,
    )
```

```python
import functools

import jax
import jax.numpy as jnp
import numpy as np
from jax import lax
from jax.experimental import pallas as pl
from jax.experimental.pallas import tpu as pltpu
from jax.sharding import PartitionSpec as P

GR = 8
SPRING = 0.25
STEP = 0.15
CHUNK = 8
PIECES = (1, 2, 3)
HALF = CHUNK // 2
BANDS = 2
HALO = 3
MESH = pl.DeviceIdType.MESH
F32 = jnp.float32
BF16 = jnp.bfloat16


def dft_tables(length):
    index = np.arange(length)
    angle = (index[:, None] * index[None, :] % length) * (2.0 * np.pi / length)
    c = np.cos(angle).astype(np.float32)
    s = np.sin(angle).astype(np.float32)
    right = np.concatenate([c, s], axis=1)
    left = np.block([[c, -s], [-s, -c]])
    inner = np.block([[c, s], [-s, c]])
    last = np.concatenate([c, -s], axis=1)
    tables = np.concatenate([right, left, inner, last], axis=0)
    return jnp.asarray(tables.astype(jnp.bfloat16))


def dot(a, b):
    return jnp.dot(a, b, preferred_element_type=F32)


def dot_nt(a, b):
    return lax.dot_general(a, b, (((1,), (1,)), ((), ())), preferred_element_type=F32)


def split3(x):
    top = x.astype(BF16)
    rest = x - top.astype(F32)
    mid = rest.astype(BF16)
    return top, mid, (rest - mid.astype(F32)).astype(BF16)


def stacked(both, a, b, side):
    ra = both[a * side : (a + 1) * side]
    rb = both[b * side : (b + 1) * side]
    top = jnp.concatenate([ra[:, :side], rb[:, :side]], axis=1)
    low = jnp.concatenate([ra[:, side:], rb[:, side:]], axis=1)
    return jnp.concatenate([top, low], axis=0)


def spectra(images, right, left):
    side = images[0].shape[0]
    rows = jnp.concatenate(images, axis=0)
    both = dot(rows, right).astype(BF16)
    return [dot(left, stacked(both, 2 * i, 2 * i + 1, side)) for i in range(len(images) // 2)]


def lane_roll(x, shift):
    return pltpu.roll(x, shift % x.shape[-1], x.ndim - 1)


def piece_of(pair, n):
    spot, middle = (pair + 1) // 2, n // 4
    size = 1 + jnp.minimum(jnp.maximum(middle + 1 - spot, 0), 2)
    return (pair % 2) * size


def up_tail(up):
    return jnp.minimum(jnp.maximum(up - 1, 0), 1)


def down_tail(up, chunks):
    return jnp.minimum(chunks - 1 - up, 1)


def up_chunks(pair, n, chunks):
    return chunks * ((pair + 1) // 2) // (n // 2)


def exchange(
    n,
    tables_any,
    list_any,
    count_s,
    tissue_any,
    patches_any,
    out_ref,
    patches_a,
    patches_b,
    tables,
    list_v,
    list_s,
    tissue_v,
    note,
    far_note,
    far_s,
    outgoing,
    incoming,
    own_spec,
    peak_ref,
    mass_ref,
    moment_ref,
    packet,
    halo,
    load_sems,
    list_sems,
    send_sems,
    recv_sems,
    halo_send,
    halo_recv,
    near_sem,
    far_sem,
):
    me = lax.axis_index("sec")
    patches = (patches_a, patches_b)
    total, _, side = patches_a.shape
    slots = list_v.shape[1]
    chunks = slots // CHUNK
    offsets = [d for d in range(-HALO, HALO + 1) if d != 0]

    loads = [
        pltpu.make_async_copy(source, target, load_sems.at[i])
        for i, (source, target) in enumerate(
            (
                (list_any, list_s),
                (list_any, list_v),
                (tables_any, tables),
                (tissue_any, tissue_v),
            )
        )
    ]
    loads[0].start()
    loads[1].start()
    bands = [pl.ds(i * side // BANDS, side // BANDS) for i in range(BANDS)]
    band_loads = [
        pltpu.make_async_copy(
            patches_any.at[0, :, band], patches[i], load_sems.at[4 + i]
        )
        for i, band in enumerate(bands)
    ]
    for load in band_loads:
        load.start()
    loads[2].start()
    loads[3].start()

    halo[...] = jnp.zeros_like(halo)
    far_note[...] = jnp.zeros_like(far_note)

    barrier = pltpu.get_barrier_semaphore()

    def greet(sem):
        for to in (me + 1 - 2 * (me % 2), me - 1 + 2 * (me % 2)):

            @pl.when((to >= 0) & (to < n))
            def _():
                pl.semaphore_signal(sem, inc=1, device_id={"sec": to}, device_id_type=MESH)

    greet(barrier)

    peak_ref[...] = jnp.zeros_like(peak_ref)
    mass_ref[...] = jnp.ones_like(mass_ref)
    moment_ref[...] = jnp.zeros_like(moment_ref)
    loads[0].wait()
    loads[1].wait()
    count = count_s[0]
    note[...] = jnp.concatenate([list_v[...], jnp.full((1, slots), count, jnp.int32)], axis=0)

    has_up = jnp.minimum(n - 1 - me, 1)
    has_down = jnp.minimum(me, 1)
    my_up = up_chunks(me, n, chunks)
    far_up = up_chunks(me - 1, n, chunks)
    my_odd, far_odd = has_up * (me % 2), has_down * (1 - me % 2)
    up_tail_to, up_tail_in = my_odd * up_tail(my_up), far_odd * up_tail(far_up)
    down_tail_in, down_tail_to = my_odd * down_tail(my_up, chunks), far_odd * down_tail(far_up, chunks)
    tail_in = up_tail_in + down_tail_in
    my_piece = has_up * piece_of(me, n)
    far_piece = has_down * piece_of(me - 1, n)
    my_half, far_half = jnp.minimum(my_piece, 1), jnp.minimum(far_piece, 1)

    sides = jnp.minimum(me, 1) + jnp.minimum(n - 1 - me, 1)
    pl.semaphore_wait(barrier, sides)

    list_copy = pltpu.make_async_remote_copy(
        src_ref=note,
        dst_ref=far_note,
        send_sem=list_sems.at[0],
        recv_sem=list_sems.at[1],
        device_id={"sec": me + 1},
        device_id_type=MESH,
    )

    slot_copy = pltpu.make_async_remote_copy(
        src_ref=list_v,
        dst_ref=far_s,
        send_sem=list_sems.at[2],
        recv_sem=list_sems.at[3],
        device_id={"sec": me + 1},
        device_id_type=MESH,
    )

    @pl.when(me < n - 1)
    def _():
        slot_copy.start()
        list_copy.start()


    def patch_copy(q, to):
        return pltpu.make_async_remote_copy(
            src_ref=outgoing.at[pl.ds(q * CHUNK, CHUNK)],
            dst_ref=incoming.at[pl.ds(q * CHUNK, CHUNK)],
            send_sem=send_sems.at[0],
            recv_sem=recv_sems.at[q],
            device_id={"sec": to},
            device_id_type=MESH,
        )

    def half_copy(q, i, to):
        at = pl.ds(q * CHUNK + i * HALF, HALF)
        return pltpu.make_async_remote_copy(
            src_ref=outgoing.at[at],
            dst_ref=incoming.at[at],
            send_sem=send_sems.at[0],
            recv_sem=recv_sems.at[2 * chunks + i],
            device_id={"sec": to},
            device_id_type=MESH,
        )

    def piece_copy(q, first, size, to):
        at = pl.ds(q * CHUNK + first, size)
        return pltpu.make_async_remote_copy(
            src_ref=outgoing.at[at],
            dst_ref=incoming.at[at],
            send_sem=send_sems.at[0],
            recv_sem=recv_sems.at[q],
            device_id={"sec": to},
            device_id_type=MESH,
        )

    def gather(source, q, c, first, count):
        for j in range(first, first + count):
            for part, band in zip(patches, bands):
                outgoing[q * CHUNK + j, band] = part[source[0, c * CHUNK + j]]

    def send_up(c, carry):
        gather(list_s, c, c, 0, CHUNK)
        patch_copy(c, me + 1).start()
        return carry

    for i, band in enumerate(bands):
        band_loads[i].wait()

        @pl.when(has_up * my_up > 0)
        def _():
            for j in range(CHUNK):
                outgoing[j, band] = patches[i][list_s[0, j]]
            pltpu.make_async_remote_copy(
                src_ref=outgoing.at[0:CHUNK, band],
                dst_ref=incoming.at[0:CHUNK, band],
                send_sem=send_sems.at[0],
                recv_sem=recv_sems.at[0],
                device_id={"sec": me + 1},
                device_id_type=MESH,
            ).start()

    n_up = has_up * my_up - up_tail_to
    lax.fori_loop(1, n_up, send_up, 0)

    for size in PIECES:

        @pl.when(my_piece == size)
        def _():
            gather(list_s, my_up, my_up, 0, size)
            piece_copy(my_up, 0, size, me + 1).start()

    @pl.when(up_tail_to > 0)
    def _():
        for i in range(2):
            gather(list_s, my_up - 1, my_up - 1, i * HALF, HALF)
            half_copy(my_up - 1, i, me + 1).start()

    greet(near_sem)
    right_ref = tables.at[0:side]
    left_ref = tables.at[side : 3 * side]
    inner_ref = tables.at[3 * side : 5 * side]
    last_ref = tables.at[5 * side : 6 * side]

    def own_group(q, carry):
        images = []
        for j in range(CHUNK):
            far = far_s[0, jnp.minimum(q, chunks - 1) * CHUNK + j]
            near = list_s[0, jnp.maximum(q - chunks, 0) * CHUNK + j]
            at = jnp.where(q < chunks, far, near)
            images.append(jnp.concatenate([part[at] for part in patches], axis=0))
        for i, spec in enumerate(spectra(images, right_ref[...], left_ref[...])):
            own_spec[q * (CHUNK // 2) + i] = spec.astype(BF16)
        return carry

    @pl.when(me > 0)
    def _():
        slot_copy.wait_recv()

    @pl.when(me == 0)
    def _():
        fill = pltpu.make_async_copy(list_v, far_s, list_sems.at[3])
        fill.start()
        fill.wait()

    for size in PIECES:

        @pl.when(far_piece == size)
        def _():
            gather(far_s, chunks + far_up, far_up, size, CHUNK - size)
            piece_copy(chunks + far_up, size, CHUNK - size, me - 1).start()

    down_from = far_up + far_half

    def send_down(c, carry):
        gather(far_s, chunks + c, c, 0, CHUNK)
        patch_copy(chunks + c, me - 1).start()
        return carry

    n_down = has_down * (chunks - down_from) - down_tail_to
    lax.fori_loop(down_from, down_from + n_down, send_down, 0)

    @pl.when(down_tail_to > 0)
    def _():
        for i in range(2):
            gather(far_s, 2 * chunks - 1, chunks - 1, i * HALF, HALF)
            half_copy(2 * chunks - 1, i, me - 1).start()

    for load in loads[2:]:
        load.wait()
    lax.fori_loop(chunks + my_up, chunks + my_up + has_up * (chunks - my_up), own_group, 0)
    lax.fori_loop(0, has_down * far_up + far_half, own_group, 0)

    pl.semaphore_wait(near_sem, sides)
    greet(far_sem)
    @pl.when(me > 0)
    def _():
        list_copy.wait_recv()

    half = side // 2
    row = lax.broadcasted_iota(jnp.int32, (side, 1), 0)
    row_lag = ((row + half) % side - half).astype(F32)
    scale = 64.0 / float(side * side * side * side)

    def match(slot, size):
        sign = jnp.where(slot < slots, -1.0, 1.0).astype(F32)
        images = [incoming[slot + j] for j in range(size)]
        crosses = []
        for i, spec in enumerate(spectra(images, right_ref[...], left_ref[...])):
            ar = spec[:side].astype(BF16).astype(F32)
            ai = spec[side:].astype(BF16).astype(F32)
            own = own_spec[slot // 2 + i].astype(F32)
            br, bi = own[:side], own[side:]
            cr = (br * ar + bi * ai).astype(BF16)
            ci = ((br * ai - bi * ar) * sign).astype(BF16)
            crosses.append(jnp.concatenate([cr[:, :side], ci[:, :side]], axis=1))
            crosses.append(jnp.concatenate([cr[:, side:], ci[:, side:]], axis=1))
        inner = dot(jnp.concatenate(crosses, axis=0), inner_ref[...]).astype(BF16)
        peaks, masses, moments = [], [], []
        for i in range(size // 2):
            scores = dot(last_ref[...], stacked(inner, 2 * i, 2 * i + 1, side)) * scale
            peak = jnp.max(scores, axis=0, keepdims=True)
            e = jnp.exp(scores - peak)
            mass = jnp.sum(e, axis=0, keepdims=True)
            moment = jnp.sum(e * row_lag, axis=0, keepdims=True)
            for parts, value in ((peaks, peak), (masses, mass), (moments, moment)):
                parts.append(value[:, :side])
                parts.append(value[:, side:])
        return [jnp.concatenate(parts, axis=0) for parts in (peaks, masses, moments)]

    def match_group(t, carry):
        start_a, count_a, start_b = carry
        q = jnp.where(t < count_a, start_a + t, start_b + t - count_a)
        skip = up_tail_in * (q < chunks).astype(jnp.int32) * (q >= far_up - 1).astype(jnp.int32)
        q = q + skip
        is_far_half = (q == far_up) & (far_half > 0)
        is_my_half = (q == chunks + my_up) & (my_half > 0)

        for size in PIECES:

            @pl.when(is_far_half & (far_piece == size))
            def _():
                piece_copy(q, 0, size, me).wait_recv()

            @pl.when(is_my_half & (my_piece == size))
            def _():
                piece_copy(q, size, CHUNK - size, me).wait_recv()

        @pl.when(jnp.logical_not(is_far_half | is_my_half))
        def _():
            patch_copy(q, me).wait_recv()

        slot = pl.multiple_of(q * CHUNK, CHUNK)
        peaks, masses, moments = match(slot, CHUNK)
        at = pl.ds(slot, CHUNK)
        peak_ref[at, :] = peaks
        mass_ref[at, :] = masses
        moment_ref[at, :] = moments
        return carry

    n_far = has_down * far_up + far_half
    n_near = has_up * (chunks - my_up)
    odd = me % 2
    start_a = (1 - odd) * (chunks + my_up)
    start_b = odd * (chunks + my_up)
    count_a = odd * n_far + (1 - odd) * n_near
    tail_q = jnp.where(up_tail_in > 0, far_up - 1, 2 * chunks - 1)
    n_main = n_far + n_near - tail_in
    lax.fori_loop(0, n_main, match_group, (start_a, count_a, start_b))

    peak = peak_ref[...]
    weight = jnp.exp(peak - jnp.max(peak, axis=1, keepdims=True))
    mass = mass_ref[...] * weight
    moment = moment_ref[...] * weight
    col = lax.broadcasted_iota(jnp.int32, (8, side), 1)
    sub = lax.broadcasted_iota(jnp.int32, (8, side), 0)
    col_lag = ((col + half) % side - half).astype(F32)
    axes = jnp.where(sub == 0, 1.0, jnp.where(sub == 1, col_lag, 0.0))
    thirds = jnp.concatenate(split3(jnp.concatenate([mass, moment], axis=0)), axis=0)
    triple = dot_nt(axes.astype(BF16), thirds)
    span = 4 * slots
    joined = triple[:, 0:span] + triple[:, span : 2 * span] + triple[:, 2 * span :]
    sums, rows_num = joined[:, 0 : 2 * slots], joined[:, 2 * slots :]
    mass_all = sums[0:1]
    place = lax.broadcasted_iota(jnp.int32, (1, 2 * slots), 1)
    is_far = place < slots
    far = far_note[...]
    counts = jnp.concatenate([far[1:2], jnp.full((1, slots), count, jnp.int32)], axis=1)
    lists = jnp.concatenate([far[0:1], list_v[...]], axis=1)
    slot = jnp.where(is_far, place, place - slots)
    first = jnp.where(is_far, 0, (chunks - n_near) * CHUNK + my_piece)
    stop = jnp.minimum(jnp.where(is_far, n_far * CHUNK - (CHUNK * far_half - far_piece), slots), counts)
    late = (place >= tail_q * CHUNK) & (place < tail_q * CHUNK + CHUNK) & (tail_in > 0)
    live = (slot >= first) & (slot < stop) & jnp.logical_not(late)
    flow_rows = jnp.where(live, rows_num[0:1] / mass_all, 0.0)
    flow_cols = jnp.where(live, sums[1:2] / mass_all, 0.0)
    which = lax.broadcasted_iota(jnp.int32, (total, 2 * slots), 0)
    onehot = (which == lists).astype(F32).astype(BF16)
    one_pair = jnp.concatenate(
        [flow_rows, flow_cols, live.astype(F32), jnp.zeros((5, 2 * slots), F32)], axis=0
    )
    both = jnp.concatenate(
        [jnp.where(is_far, one_pair, 0.0), jnp.where(is_far, 0.0, one_pair)], axis=0
    )
    triple = dot_nt(jnp.concatenate(split3(both), axis=0), onehot)
    field = triple[0:16] + triple[16:32] + triple[32:48]
    packet[0:3] = field[0:3]
    packet[3:4] = tissue_v[...].astype(F32)
    packet[4:8] = field[4:8]
    packet[8:16] = field[8:16]
    packet[4:5, 0 : 2 * slots] = flow_rows
    packet[5:6, 0 : 2 * slots] = flow_cols

    lane = lax.broadcasted_iota(jnp.int32, (HALF, side), 1)
    step = lax.broadcasted_iota(jnp.int32, (HALF, side), 0)
    late_lag = ((lane + half) % side - half).astype(F32)
    spot = lax.broadcasted_iota(jnp.int32, (HALF, total), 1)
    turn = lax.broadcasted_iota(jnp.int32, (HALF, total), 0)
    late_far = up_tail_in > 0
    late_count = jnp.where(late_far, far_note[1:2, 0:1], jnp.full((1, 1), count, jnp.int32))

    def match_tail(i, carry):
        for k in range(2):

            @pl.when(i == k)
            def _():
                half_copy(tail_q, k, me).wait_recv()

        at = pl.multiple_of(tail_q * CHUNK + i * HALF, HALF)
        peak, mass, moment = match(at, HALF)
        weight = jnp.exp(peak - jnp.max(peak, axis=1, keepdims=True))
        mass = mass * weight
        whole = jnp.sum(mass, axis=1, keepdims=True)
        rows = jnp.sum(moment * weight, axis=1, keepdims=True) / whole
        cols = jnp.sum(mass * late_lag, axis=1, keepdims=True) / whole
        own_at = jnp.where(late_far, at, at - slots)
        ids = jnp.zeros((HALF, total), jnp.int32)
        for j in range(HALF):
            listed = jnp.where(late_far, far_s[0, own_at + j], list_s[0, own_at + j])
            ids = jnp.where(turn == j, listed, ids)
        alive = turn + own_at < late_count
        hit = (spot == ids) & alive
        here = (spot == turn + at) & alive
        picks = [
            jnp.where(hit, rows, 0.0),
            jnp.where(hit, cols, 0.0),
            hit.astype(F32),
            jnp.where(here, rows, 0.0),
            jnp.where(here, cols, 0.0),
        ]
        picks = [jnp.sum(pick, axis=0, keepdims=True) for pick in picks]
        blank = jnp.zeros((1, total), F32)
        field = jnp.concatenate(picks[:3] + [blank] * 5, axis=0)
        flows = jnp.concatenate([blank] * 4 + picks[3:] + [blank] * 2, axis=0)
        packet[0:8] = packet[0:8] + (jnp.where(late_far, field, 0.0) + flows)
        packet[8:16] = packet[8:16] + jnp.where(late_far, 0.0, field)
        return carry

    pl.semaphore_wait(far_sem, sides)
    lax.fori_loop(0, 2 * tail_in, match_tail, 0)

    def halo_copy(d):
        return pltpu.make_async_remote_copy(
            src_ref=packet,
            dst_ref=halo.at[HALO - d],
            send_sem=halo_send.at[0],
            recv_sem=halo_recv.at[(HALO - d) - (d < 0)],
            device_id={"sec": me + d},
            device_id_type=MESH,
        )

    for d in offsets:

        @pl.when((me + d >= 0) & (me + d < n))
        def _():
            halo_copy(d).start()

    @pl.when(me < n - 1)
    def _():
        slot_copy.wait_send()
        list_copy.wait_send()

    def drain_up(c, carry):
        patch_copy(c, me + 1).wait_send()
        return carry

    lax.fori_loop(0, n_up, drain_up, 0)

    @pl.when(up_tail_to > 0)
    def _():
        for i in range(2):
            half_copy(my_up - 1, i, me + 1).wait_send()

    for size in PIECES:

        @pl.when(my_piece == size)
        def _():
            piece_copy(my_up, 0, size, me + 1).wait_send()

    def drain_down(c, carry):
        patch_copy(chunks + c, me - 1).wait_send()
        return carry

    lax.fori_loop(down_from, down_from + n_down, drain_down, 0)

    @pl.when(down_tail_to > 0)
    def _():
        for i in range(2):
            half_copy(2 * chunks - 1, i, me - 1).wait_send()

    for size in PIECES:

        @pl.when(far_piece == size)
        def _():
            piece_copy(chunks + far_up, size, CHUNK - size, me - 1).wait_send()

    for d in offsets:

        @pl.when((me - d >= 0) & (me - d < n))
        def _():
            halo_copy(d).wait_recv()

    halo[HALO] = packet[...]
    relax(slots, halo, out_ref)
    for d in offsets:

        @pl.when((me + d >= 0) & (me + d < n))
        def _():
            halo_copy(d).wait_send()


def relax(slots, halo, out_ref):
    total = halo.shape[-1]
    near, above = halo[HALO], halo[HALO + 1]
    out_ref[2:4, 0:slots] = near[4:6, slots : 2 * slots] + above[4:6, 0:slots]
    fields = {d: halo[HALO + d][8:16] + halo[HALO + d + 1][0:8] for d in range(-HALO, HALO)}
    links = {d: jnp.broadcast_to(f[2:3], f.shape) for d, f in fields.items()}
    lane = lax.broadcasted_iota(jnp.int32, (8, total), 1)
    width = total // GR
    has_right = (lane % width) != width - 1
    has_below = lane < total - width

    def springs(d):
        tissue = jnp.broadcast_to(halo[HALO + d][3:4], (8, total))
        stiff = SPRING * (1.0 + 2.0 * tissue)
        across = jnp.where(has_right, 0.5 * (stiff + lane_roll(stiff, -1)), 0.0)
        along = jnp.where(has_below, 0.5 * (stiff + lane_roll(stiff, -width)), 0.0)
        return across, along

    def plane(u, spring):
        across, along = spring
        a = across * (lane_roll(u, -1) - u)
        b = along * (lane_roll(u, -width) - u)
        return (lane_roll(a, 1) - a) + (lane_roll(b, width) - b)

    spring = {d: springs(d) for d in (-1, 0, 1)}
    pull = {d: links[d] * fields[d] for d in fields}
    u1 = {d: -STEP * (pull[d] - pull[d - 1]) for d in range(-2, 3)}

    def relaxed(u, d):
        gap_here = u[d + 1] - u[d] - fields[d]
        gap_below = u[d] - u[d - 1] - fields[d - 1]
        force = plane(u[d], spring[d]) - links[d] * gap_here + links[d - 1] * gap_below
        return u[d] - STEP * force

    u2 = {d: relaxed(u1, d) for d in (-1, 0, 1)}
    out_ref[0:2] = relaxed(u2, 0)[0:2]


def unpack(both, flow_ref, pos_ref):
    flow_ref[0] = both[2:4, 0 : flow_ref.shape[-1]]
    pos_ref[0] = both[0:2]


def on_device(n, patches, pair_list, pair_count, tissue):
    _, total, side, _ = patches.shape
    slots = pair_list.shape[1]
    chunks = slots // CHUNK
    vmem = pl.BlockSpec(memory_space=pltpu.VMEM)
    any_space = pl.BlockSpec(memory_space=pl.ANY)
    dma = pltpu.SemaphoreType.DMA
    both = pl.pallas_call(
        functools.partial(exchange, n),
        out_shape=pltpu.VMEM((4, total), F32),
        in_specs=[any_space] * 2 + [pl.BlockSpec(memory_space=pltpu.SMEM)] + [any_space] * 2,
        out_specs=vmem,
        scratch_shapes=[
            pltpu.VMEM((total, side // BANDS, side), BF16),
            pltpu.VMEM((total, side // BANDS, side), BF16),
            pltpu.VMEM((6 * side, 2 * side), BF16),
            pltpu.VMEM((1, slots), jnp.int32),
            pltpu.SMEM((1, slots), jnp.int32),
            pltpu.VMEM((1, total), jnp.int32),
            pltpu.VMEM((2, slots), jnp.int32),
            pltpu.VMEM((2, slots), jnp.int32),
            pltpu.SMEM((1, slots), jnp.int32),
            pltpu.VMEM((2 * slots, side, side), BF16),
            pltpu.VMEM((2 * slots, side, side), BF16),
            pltpu.VMEM((slots, 2 * side, 2 * side), BF16),
            pltpu.VMEM((2 * slots, side), F32),
            pltpu.VMEM((2 * slots, side), F32),
            pltpu.VMEM((2 * slots, side), F32),
            pltpu.VMEM((16, total), F32),
            pltpu.VMEM((2 * HALO + 1, 16, total), F32),
            dma((4 + BANDS,)),
            dma((4,)),
            dma((1,)),
            dma((2 * chunks + 2,)),
            dma((1,)),
            dma((2 * HALO,)),
            pltpu.SemaphoreType.REGULAR,
            pltpu.SemaphoreType.REGULAR,
        ],
        compiler_params=pltpu.CompilerParams(
            collective_id=0, has_side_effects=True, vmem_limit_bytes=64_000_000
        ),
        name="exchange",
    )(dft_tables(side), pair_list, pair_count, tissue, patches)
    return pl.pallas_call(
        unpack,
        out_shape=(
            jax.ShapeDtypeStruct((1, 2, slots), F32),
            jax.ShapeDtypeStruct((1, 2, total), F32),
        ),
        in_specs=[vmem],
        out_specs=(vmem, vmem),
        compiler_params=pltpu.CompilerParams(vmem_limit_bytes=2_000_000),
        name="unpack",
    )(both)


def solution(mesh):
    return jax.shard_map(
        functools.partial(on_device, mesh.shape["sec"]),
        mesh=mesh,
        in_specs=(
            P(("group", "sec"), None, None, None),
            P(("group", "sec"), None),
            P(("group", "sec")),
            P(("group", "sec"), None),
        ),
        out_specs=(P(("group", "sec"), None, None), P(("group", "sec"), None, None)),
        check_vma=False,
    )
```
